256 devices in a mesh: sec: 4 (over z_lo), band: 32 (over y, z_hi, x), ch: 2 (over core).
Axes of the slice: x: 4, y: 4, z: 8 (z_hi: 2, z_lo: 4; z = z_hi * 4 + z_lo), core: 2. Of those that a mesh axis runs over, the one named last changes fastest.
Arguments:
- air_field_lattice: bfloat16 [512, 1024, 768], P(('sec', 'band', 'ch')), may hold values from -6 to 6
- associated_polynomial_matrix: bfloat16 [512, 512, 512], P(('sec', 'band', 'ch')), may hold values from -0.25 to 0.25
- harmonic_damping_factor: float32 [512, 768], replicated, may hold values from 0.5 to 2
- boundary_exchange_projector: bfloat16 [768, 8], replicated, may hold values from -0.21875 to 0.21875
- warmth_response_factor: float32 [768], replicated, may hold values from -4 to 4
- water_patch_fields: bfloat16 [1536, 128, 4, 258], P(('sec', 'band', 'ch')), may hold values from -6 to 6
- kernel_coefficients: bfloat16 [3, 3, 128, 128], replicated, may hold values from -0.1875 to 0.1875
- local_exchange_matrix: bfloat16 [8, 128], replicated, may hold values from -2 to 2
- patch_average_matrix: float32 [8, 128], replicated, may hold values from -15 to 15
- water_kernel_offset: float32 [128], replicated, may hold values from -3 to 3
- water_readout_matrix: bfloat16 [128, 128], replicated, may hold values from -0.5 to 0.5
- patch_holder_index: int32 [256, 4], replicated, may hold values from 0 to 31, as said below
- water_point_indicator: int32 [1536, 2, 256], P(('sec', 'band', 'ch')), may hold values from 0 to 1, as said below
- water_point_totals: int32 [1536], P(('sec', 'band', 'ch')), may hold values from 0 to 512, as said below
Outputs:
- advanced_air_field: bfloat16 [512, 1024, 768], P(('sec', 'band', 'ch'))
- ocean_next: bfloat16 [1536, 128, 2, 256], P(('sec', 'band', 'ch'))
The draws below stay inside these ranges and needn't reach their ends.
Inputs may be any that keep to these rules, and one draw needn't show every extreme that they name: `patch_holder_index`: within each group of equal s and c, every band index owns either 6 or 2 of the group's tiles, half of them each way, so no device owns more than 6. `water_point_indicator`: empty slots are all zeros. `water_point_totals`: the number of ones of the slot in water_point_indicator.
All inputs are finite; a program needn't handle non-finite values.
Results may differ from the reference program's by a relative error of at most 0.0058.
Values may be sent and summed in bfloat16 or wider, within the bound.
A program may use at most 128 MiB of HBM per device.

```python
import math
import jax
import jax.numpy as jnp
from jax import lax

LATD = 2
MERIDIANS = 1024
AIR_FEATURES = 768
K = 512
NF = 8
OCH = 128
TPR = 4
TSLOT = 6
TW = 256
PARALLELS = 512
OSLOTS = 1536
N_SEC = 4
N_BAND = 32
N_CH = 2
DEVICES = 256


def owner_layout(key):
    group_total = N_SEC * N_CH
    group_keys = jax.random.split(jax.random.fold_in(key, 11), group_total)

    def one_group(group_key):
        first_key, second_key = jax.random.split(group_key)
        heavy = jax.random.permutation(first_key, N_BAND) < N_BAND // 2
        counts = jnp.where(heavy, TPR + TPR // 2, TPR - TPR // 2).astype(jnp.int32)
        bounds = jnp.cumsum(counts)
        tile_index = jnp.arange(N_BAND * TPR, dtype=jnp.int32)
        sequence = jnp.sum((bounds[None, :] <= tile_index[:, None]).astype(jnp.int32), axis=1)
        shuffle = jax.random.permutation(second_key, N_BAND * TPR)
        return (sequence[shuffle].astype(jnp.int32), counts)
    owners, counts = jax.vmap(one_group)(group_keys)
    owners = owners.reshape(N_SEC, N_CH, N_BAND, TPR).transpose(0, 2, 1, 3).reshape(N_SEC * N_BAND * N_CH, TPR)
    counts = counts.reshape(N_SEC, N_CH, N_BAND).transpose(0, 2, 1).reshape(-1)
    return (owners, counts)


def wet_layout(key):
    owners, counts = owner_layout(key)
    mask_key = jax.random.fold_in(key, 23)
    kind_key, level_key, cell_key = jax.random.split(mask_key, 3)
    slot_total = N_SEC * N_BAND * N_CH * TSLOT
    live = (jnp.arange(TSLOT, dtype=jnp.int32)[None, :] < counts[:, None]).reshape(-1)
    kind = jax.random.randint(kind_key, (slot_total,), 0, 8)
    level = jax.random.randint(level_key, (slot_total,), 300, 1001)
    level = jnp.where(kind == 0, 0, jnp.where(kind == 1, 1000, level))
    cell_draw = jax.random.randint(cell_key, (slot_total, LATD, TW), 0, 1000)
    wet = ((cell_draw < level[:, None, None]) & live[:, None, None]).astype(jnp.int32)
    return (wet, jnp.sum(wet, axis=(1, 2)).astype(jnp.int32))


def draw_patch_holder_index(key, part):
    return owner_layout(key)[0]


def draw_water_point_indicator(key, part):
    return wet_layout(key)[0]


def draw_water_point_totals(key, part):
    return wet_layout(key)[1]


def block_levels(rng, extent, shards, smallest, top_value):
    gain, own = 1.0, jax.random.fold_in(rng, 6)
    for axis_at, blocks in shards:
        heights = jnp.exp(jax.random.uniform(jax.random.fold_in(own, axis_at), (blocks,), jnp.float32, smallest / len(shards), top_value / len(shards)))
        gain = gain * jnp.repeat(heights, extent[axis_at] // blocks).reshape([-1 if axis == axis_at else 1 for axis in range(len(extent))])
    return gain


def scatter_about(key, dims, spread, reach, cuts=(), kind=jnp.bfloat16):
    result = jax.random.normal(key, dims, jnp.float32) * spread
    if len(cuts) > 0:
        result = block_levels(key, dims, cuts, -0.22, 0.18) * result
    return jnp.clip(result, min=-reach, max=reach).astype(kind)


def setup_inputs(seed: int = 0) -> dict:
    splits = jax.random.split(jax.random.key(seed), 15)
    air_field_lattice = scatter_about(splits[0], (PARALLELS, MERIDIANS, AIR_FEATURES), 1.0, 6.0, ((0, 256),))
    associated_polynomial_matrix = scatter_about(splits[1], (K, PARALLELS, PARALLELS), PARALLELS ** -0.5, 0.25, ((0, 256),))
    harmonic_damping_factor = jnp.clip(jnp.exp(jax.random.uniform(splits[2], (PARALLELS, AIR_FEATURES), jnp.float32, math.log(0.5), math.log(2.0))), 0.5, 2.0)
    boundary_exchange_projector = scatter_about(splits[3], (AIR_FEATURES, NF), AIR_FEATURES ** -0.5, 0.21875)
    warmth_response_factor = scatter_about(splits[4], (AIR_FEATURES,), 1.0, 4.0, (), jnp.float32)
    water_patch_fields = scatter_about(splits[5], (OSLOTS, OCH, LATD + 2, TW + 2), 1.0, 6.0, ((0, 256),))
    kernel_coefficients = scatter_about(splits[6], (3, 3, OCH, OCH), (9 * OCH) ** -0.5, 0.1875)
    local_exchange_matrix = scatter_about(splits[7], (NF, OCH), NF ** -0.5, 2.0)
    patch_average_matrix = scatter_about(splits[8], (NF, OCH), 3.0, 15.0, (), jnp.float32)
    water_kernel_offset = scatter_about(splits[9], (OCH,), 0.5, 3.0, (), jnp.float32)
    water_readout_matrix = scatter_about(splits[10], (OCH, OCH), OCH ** -0.5, 0.5)
    patch_holder_index = draw_patch_holder_index(jax.random.fold_in(splits[14], 71), 0)
    water_point_indicator = draw_water_point_indicator(jax.random.fold_in(splits[14], 71), 0)
    water_point_totals = draw_water_point_totals(jax.random.fold_in(splits[14], 71), 0)
    return {"air_field_lattice": air_field_lattice, "associated_polynomial_matrix": associated_polynomial_matrix, "harmonic_damping_factor": harmonic_damping_factor, "boundary_exchange_projector": boundary_exchange_projector, "warmth_response_factor": warmth_response_factor, "water_patch_fields": water_patch_fields, "kernel_coefficients": kernel_coefficients, "local_exchange_matrix": local_exchange_matrix, "patch_average_matrix": patch_average_matrix, "water_kernel_offset": water_kernel_offset, "water_readout_matrix": water_readout_matrix, "patch_holder_index": patch_holder_index, "water_point_indicator": water_point_indicator, "water_point_totals": water_point_totals}


def dft_tables(meridian_number, column_order):
    cell_index = jnp.arange(meridian_number, dtype=jnp.int32)[:, None]
    wavenumber = (column_order // 2)[None, :]
    component = (column_order % 2)[None, :]
    phase_angle = ((cell_index * wavenumber) % meridian_number).astype(jnp.float32) * (2.0 * math.pi / meridian_number)
    basis_table = jnp.where(component == 0, jnp.cos(phase_angle), -jnp.sin(phase_angle))
    forward = basis_table.astype(jnp.bfloat16)
    inverse = (basis_table.T * (2.0 / meridian_number)).astype(jnp.bfloat16)
    return forward, inverse


def ocean_update(state, tile_flux, mask_tile, count_tile, kernel_coefficients, local_exchange_matrix, patch_average_matrix, water_kernel_offset, water_readout_matrix):
    mask_f = mask_tile.astype(jnp.float32)
    masked = tile_flux.astype(jnp.float32) * mask_f[:, None]
    fmean = jnp.sum(masked, axis=(2, 3)) / jnp.maximum(count_tile.astype(jnp.float32), 1.0)[:, None]
    state_f = state.astype(jnp.float32)
    total = jnp.einsum('fo,sfrw->sorw', local_exchange_matrix.astype(jnp.float32), masked)
    for shift_row in range(3):
        for shift_col in range(3):
            window = state_f[:, :, shift_row:shift_row + LATD, shift_col:shift_col + TW]
            total = total + jnp.einsum('io,sirw->sorw', kernel_coefficients[shift_row, shift_col].astype(jnp.float32), window)
    mean_term = jnp.sum(fmean[:, :, None] * patch_average_matrix[None], axis=1)
    total = total + mean_term[:, :, None, None] + water_kernel_offset[None, :, None, None]
    hidden = jax.nn.gelu(total, approximate=True).astype(jnp.bfloat16)
    update = jnp.einsum('io,sirw->sorw', water_readout_matrix.astype(jnp.float32), hidden.astype(jnp.float32))
    fresh = (state_f[:, :, 1:1 + LATD, 1:1 + TW] + update) * mask_f[:, None]
    return fresh.astype(jnp.bfloat16)


def reference(air_field_lattice, associated_polynomial_matrix, harmonic_damping_factor, boundary_exchange_projector, warmth_response_factor, water_patch_fields, kernel_coefficients, local_exchange_matrix, patch_average_matrix, water_kernel_offset, water_readout_matrix, patch_holder_index, water_point_indicator, water_point_totals):
    column_order = jnp.arange(2 * K, dtype=jnp.int32)
    forward, inverse = dft_tables(MERIDIANS, column_order)
    forward_f = forward.astype(jnp.float32)
    inverse_f = inverse.astype(jnp.float32)

    def analyse(parallel_line):
        return jnp.dot(forward_f.T, parallel_line.astype(jnp.float32)).astype(jnp.bfloat16)

    fourier = lax.map(analyse, air_field_lattice)
    paired = jnp.moveaxis(fourier.reshape(PARALLELS, K, 2, AIR_FEATURES), 0, 1)

    def latitudinal(operands):
        matrix, coeffs = operands
        matrix_f = matrix.astype(jnp.float32)
        spectrum = jnp.einsum('lt,tpc->lpc', matrix_f, coeffs.astype(jnp.float32))
        scaled = (spectrum * harmonic_damping_factor[:, None, :]).astype(jnp.bfloat16)
        return jnp.einsum('lt,lpc->tpc', matrix_f, scaled.astype(jnp.float32)).astype(jnp.bfloat16)

    damped_modes = lax.map(latitudinal, (associated_polynomial_matrix, paired))
    damped_modes = jnp.moveaxis(damped_modes, 0, 1).reshape(PARALLELS, 2 * K, AIR_FEATURES)

    flux_f = boundary_exchange_projector.astype(jnp.float32)

    def surface(parallel_line):
        return jnp.dot(parallel_line.astype(jnp.float32), flux_f).T.astype(jnp.bfloat16)

    flux_rows = lax.map(surface, air_field_lattice)
    grouped = flux_rows.reshape(N_SEC, N_BAND, N_CH, LATD, NF, TPR, TW).transpose(0, 2, 1, 5, 4, 3, 6)
    grouped = grouped.reshape(N_SEC, N_CH, N_BAND * TPR, NF, LATD, TW).astype(jnp.float32)

    owner_grid = patch_holder_index.reshape(N_SEC, N_BAND, N_CH, TPR)
    group_tiles = owner_grid.transpose(0, 2, 1, 3).reshape(N_SEC, N_CH, N_BAND * TPR)
    holders = jnp.arange(N_BAND, dtype=jnp.int32)
    mine = group_tiles[:, :, None, :] == holders[None, None, :, None]
    ranks = jnp.cumsum(mine.astype(jnp.int32), axis=-1) - 1
    slot_index = jnp.arange(TSLOT, dtype=jnp.int32)
    chooser = (mine[:, :, :, None, :] & (ranks[:, :, :, None, :] == slot_index[None, None, None, :, None])).astype(jnp.float32)
    tile_flux = jnp.einsum('scbit,sctfrw->sbcifrw', chooser, grouped)
    tile_flux = tile_flux.reshape(DEVICES, TSLOT, NF, LATD, TW).astype(jnp.bfloat16)

    def ocean_device(operands):
        state, flux_tile, mask_tile, count_tile = operands
        return ocean_update(state, flux_tile, mask_tile, count_tile, kernel_coefficients, local_exchange_matrix, patch_average_matrix, water_kernel_offset, water_readout_matrix)

    ocean_next = lax.map(ocean_device, (water_patch_fields.reshape(DEVICES, TSLOT, OCH, LATD + 2, TW + 2), tile_flux, water_point_indicator.reshape(DEVICES, TSLOT, LATD, TW), water_point_totals.reshape(DEVICES, TSLOT)))

    sea_slots = ocean_next[:, :, 0].reshape(N_SEC, N_BAND, N_CH, TSLOT, LATD, TW)
    rank_tile = jnp.sum(jnp.where(mine, ranks, 0), axis=2)
    rank_grid = rank_tile.reshape(N_SEC, N_CH, N_BAND, TPR).transpose(0, 2, 1, 3)
    sec_idx = jnp.arange(N_SEC, dtype=jnp.int32)[:, None, None, None]
    core_idx = jnp.arange(N_CH, dtype=jnp.int32)[None, None, :, None]
    chosen_entries = sea_slots[sec_idx, owner_grid, core_idx, rank_grid]
    water_skin_warmth = chosen_entries.transpose(0, 1, 2, 4, 3, 5).reshape(PARALLELS, MERIDIANS)

    def merge_parts(operands):
        coeffs, parallel_line, water_line = operands
        reconstruct_physical = jnp.dot(inverse_f.T, coeffs.astype(jnp.float32))
        advanced_pair = parallel_line.astype(jnp.float32) + reconstruct_physical + water_line.astype(jnp.float32)[:, None] * warmth_response_factor[None, :]
        return advanced_pair.astype(jnp.bfloat16)

    advanced_air_field = lax.map(merge_parts, (damped_modes, air_field_lattice, water_skin_warmth))
    return advanced_air_field, ocean_next.reshape(OSLOTS, OCH, LATD, TW)
```

```python
import functools
import math

import jax
import jax.numpy as jnp
import numpy as np
from jax import lax
from jax.experimental import pallas as pl
from jax.experimental.pallas import tpu as pltpu
from jax.sharding import PartitionSpec as P

MESH = pl.DeviceIdType.MESH
CHUNKS = (256, 256, 256)
NZ, NY, NX, NC = 8, 4, 4, 2
NP = NY * NX * NC
N = 1024
LAT = 512


def trig(a, b):
    phase = (a[:, None].astype(np.int64) * b[None, :]) % N
    angle = phase.astype(np.float64) * (2.0 * math.pi / N)
    return np.cos(angle).astype(np.float32), np.sin(angle).astype(np.float32)


def basis_tables():
    n = np.arange(N)
    zh, zl, part, y = np.meshgrid(np.arange(2), np.arange(4), np.arange(2), np.arange(4), indexing="ij")
    k_hi = (zl * 128 + y * 32 + zh * 16).reshape(-1)
    part_hi = part.reshape(-1)[:, None]
    k_lo = np.arange(16)
    ch, sh = trig(k_hi, n)
    cl, sl = trig(k_lo, n)
    u1 = np.where(part_hi == 0, ch, -sh)
    u2 = np.where(part_hi == 0, -sh, -ch)
    fwd = jnp.asarray(u1)[:, None, :] * jnp.asarray(cl)[None] + jnp.asarray(u2)[:, None, :] * jnp.asarray(sl)[None]
    fwd = fwd.astype(jnp.bfloat16).reshape(N, N)
    k_all = (k_hi[:, None] + k_lo[None, :]).reshape(-1)
    part_all = np.repeat(part.reshape(-1), 16)[None, :]
    c1, s1 = trig(np.arange(32) * 32, k_all)
    c0, s0 = trig(np.arange(32), k_all)
    v1 = np.where(part_all == 0, c1, -s1)
    v2 = np.where(part_all == 0, -s1, -c1)
    inv = jnp.asarray(v1)[:, None, :] * jnp.asarray(c0)[None] + jnp.asarray(v2)[:, None, :] * jnp.asarray(s0)[None]
    inv = inv.astype(jnp.bfloat16).reshape(N, N)
    return fwd, inv


def one_hot(rows, cols, fn):
    r = lax.broadcasted_iota(jnp.int32, (rows, cols), 0)
    c = lax.broadcasted_iota(jnp.int32, (rows, cols), 1)
    return jnp.where(fn(r, c), 1.0, 0.0).astype(jnp.bfloat16)


def true_lat(i):
    t = i & 1
    z_lo = (i >> 1) & 3
    z_hi = (i >> 3) & 1
    c = (i >> 4) & 1
    x = (i >> 5) & 3
    y = (i >> 7) & 3
    return (z_lo * 64 + y * 16 + z_hi * 8 + x * 2 + c) * 2 + t


def spectral_kernel(
    air_hbm, fwd_hbm, inv_hbm, pol_hbm, damp_hbm, warm_ref, sea_ref, out_hbm, *scr
):
    nchunk = len(CHUNKS)
    it = iter(scr)
    fwd, inv, pol, polp, polt, damp, q1, q2 = (next(it) for _ in range(8))
    airv = [next(it) for _ in CHUNKS]
    zs1 = [next(it) for _ in CHUNKS]
    zr1 = [next(it) for _ in CHUNKS]
    ps1 = [next(it) for _ in CHUNKS]
    mid = [next(it) for _ in CHUNKS]
    ret = [next(it) for _ in CHUNKS]
    pr2 = [next(it) for _ in CHUNKS]
    zs2 = [next(it) for _ in CHUNKS]
    fin = [next(it) for _ in CHUNKS]
    load_sem, out_sem, send_sem, recv_sem, self_sem = (next(it) for _ in range(5))

    s = lax.axis_index("sec")
    b = lax.axis_index("band")
    c = lax.axis_index("ch")
    y = b // 8
    z_hi = lax.rem(b // 4, 2)
    x = lax.rem(b, 4)
    z = z_hi * 4 + s
    p = y * 8 + x * 2 + c

    def z_dev(zz):
        return (lax.rem(zz, 4), y * 8 + (zz // 4) * 4 + x, c)

    def p_dev(pp):
        return (s, (pp // 8) * 8 + z_hi * 4 + lax.rem(pp // 2, 4), lax.rem(pp, 2))

    offs = [0]
    for w in CHUNKS:
        offs.append(offs[-1] + w)

    loads = []

    def load(src, dst):
        copy = pltpu.make_async_copy(src, dst, load_sem.at[len(loads)])
        copy.start()
        loads.append(copy)
        return copy

    ld_fwd = load(fwd_hbm, fwd)
    ld_air = [load(air_hbm.at[:, :, pl.ds(offs[j], CHUNKS[j])], airv[j]) for j in range(nchunk)]
    ld_pol = load(pol_hbm, pol)
    ld_damp = load(damp_hbm, damp)
    ld_inv = load(inv_hbm, inv)

    barrier = pltpu.get_barrier_semaphore()

    def greet_z(i, _):
        pl.semaphore_signal(barrier, inc=1, device_id=z_dev(lax.rem(z + i, NZ)), device_id_type=MESH)
        return 0

    def greet_p(i, _):
        pl.semaphore_signal(barrier, inc=1, device_id=p_dev(lax.rem(p + i, NP)), device_id_type=MESH)
        return 0

    lax.fori_loop(1, NZ, greet_z, 0)
    lax.fori_loop(1, NP, greet_p, 0)

    def z_copy(stage, j, src, dst, i):
        to = lax.rem(z + i, NZ)
        return pltpu.make_async_remote_copy(
            src_ref=src.at[to], dst_ref=dst.at[z],
            send_sem=send_sem.at[stage, j], recv_sem=recv_sem.at[stage, j],
            device_id=z_dev(to), device_id_type=MESH,
        )

    def z_start(stage, j, src, dst):
        pltpu.make_async_copy(src.at[z], dst.at[z], self_sem.at[stage, j]).start()

        def go(i, _):
            z_copy(stage, j, src, dst, i).start()
            return 0

        lax.fori_loop(1, NZ, go, 0)

    def z_wait(stage, j, src, dst):
        pltpu.make_async_copy(src.at[z], dst.at[z], self_sem.at[stage, j]).wait()
        pltpu.make_async_copy(src.at[pl.ds(0, NZ - 1)], dst.at[pl.ds(0, NZ - 1)], recv_sem.at[stage, j]).wait()

    def z_sent(stage, j, src, dst):
        pltpu.make_async_copy(src.at[pl.ds(0, NZ - 1)], dst.at[pl.ds(0, NZ - 1)], send_sem.at[stage, j]).wait()

    def p_start(stage, j, src, dst):
        def pick(to):
            if stage == 1:
                return src.at[to], dst.at[:, :, p]
            return src.at[:, :, to], dst.at[p]

        a, d = pick(p)
        pltpu.make_async_copy(a, d, self_sem.at[stage, j]).start()

        def go(i, _):
            to = lax.rem(p + i, NP)
            a, d = pick(to)
            pltpu.make_async_remote_copy(
                src_ref=a, dst_ref=d, send_sem=send_sem.at[stage, j], recv_sem=recv_sem.at[stage, j],
                device_id=p_dev(to), device_id_type=MESH,
            ).start()
            return 0

        lax.fori_loop(1, NP, go, 0)

    def p_wait(stage, j, flat, whole):
        a = flat.at[0]
        pltpu.make_async_copy(a, a, self_sem.at[stage, j]).wait()
        a = flat.at[pl.ds(0, NP - 1)]
        pltpu.make_async_copy(a, a, recv_sem.at[stage, j]).wait()

    def p_sent(stage, j, flat):
        a = flat.at[pl.ds(0, NP - 1)]
        pltpu.make_async_copy(a, a, send_sem.at[stage, j]).wait()

    def dot(a, bb):
        return jnp.dot(a, bb, preferred_element_type=jnp.float32)

    def dft(j):
        w = CHUNKS[j]

        def body(i, _):
            t = i // 4
            m = lax.rem(i, 4)
            rows = fwd[pl.ds(pl.multiple_of(m * 256, 256), 256), :]
            f = dot(rows, airv[j][t]).astype(jnp.bfloat16)
            zs1[j][pl.ds(m * 2, 2), t] = f.reshape(2, 128, w)
            return 0

        lax.fori_loop(0, 8, body, 0)

    def perm1(j):
        w = CHUNKS[j]

        def body(i, _):
            part = i // 4
            g = lax.rem(i, 4)
            r0 = pl.multiple_of(part * 64 + g * 16, 16)
            xin = zr1[j][:, :, pl.ds(r0, 16), :].reshape(256, w)
            yo = dot(q1[...], xin).astype(jnp.bfloat16)
            ps1[j][pl.ds(g * 8, 8), part] = yo.reshape(8, 2, 16, w)
            return 0

        lax.fori_loop(0, 8, body, 0)

    def middle(j):
        w = CHUNKS[j]
        d0 = offs[j]

        def body(i, _):
            part = i // 2
            k = lax.rem(i, 2)
            xin = mid[j][part, k].reshape(LAT, w)
            sp = dot(polp[k], xin)
            sc = (sp * damp[:, d0:d0 + w]).astype(jnp.bfloat16)
            fo = dot(polt[k], sc).astype(jnp.bfloat16)
            ret[j][part, k] = fo.reshape(NP, 16, w)
            return 0

        lax.fori_loop(0, 4, body, 0)

    def perm2(j):
        w = CHUNKS[j]

        def body(i, _):
            part = i // 4
            g = lax.rem(i, 4)
            r0 = pl.multiple_of(part * 64 + g * 16, 16)
            xin = pr2[j][pl.ds(g * 8, 8), part].reshape(256, w)
            yo = dot(q2[...], xin).astype(jnp.bfloat16)
            zs2[j][:, :, pl.ds(r0, 16), :] = yo.reshape(8, 2, 16, w)
            return 0

        lax.fori_loop(0, 8, body, 0)

    def inverse(j):
        w = CHUNKS[j]
        d0 = offs[j]

        def body(i, _):
            t = i // 4
            m = pl.multiple_of(lax.rem(i, 4) * 256, 256)
            rows = inv[pl.ds(m, 256), :]
            rec = dot(rows, fin[j][:, t].reshape(N, w)) * (1.0 / 512.0)
            old = airv[j][t, pl.ds(m, 256), :].astype(jnp.float32)
            sea = sea_ref[t, pl.ds(m, 256), :]
            new = old + rec + sea * warm_ref[:, d0:d0 + w]
            airv[j][t, pl.ds(m, 256), :] = new.astype(jnp.bfloat16)
            return 0

        lax.fori_loop(0, 8, body, 0)
        pltpu.make_async_copy(airv[j], out_hbm.at[:, :, pl.ds(d0, w)], out_sem.at[j]).start()

    def prepare():
        q1[...] = one_hot(256, 256, lambda r, q: (((r & 15) == (q >> 4)) & ((r >> 5) == ((q >> 1) & 7)) & (((r >> 4) & 1) == (q & 1))))
        q2[...] = one_hot(256, 256, lambda q, r: (((r & 15) == (q >> 4)) & ((r >> 5) == ((q >> 1) & 7)) & (((r >> 4) & 1) == (q & 1))))
        ld_pol.wait()
        sel = one_hot(LAT, LAT, lambda r, q: r == true_lat(q))
        selt = one_hot(LAT, LAT, lambda r, q: true_lat(r) == q)
        for k in range(2):
            polp[k] = dot(pol[k], sel).astype(jnp.bfloat16)
            polt[k] = lax.dot_general(
                selt, pol[k], (((1,), (1,)), ((), ())), preferred_element_type=jnp.float32
            ).astype(jnp.bfloat16)
        ld_damp.wait()

    last = nchunk - 1
    ld_fwd.wait()
    ld_air[0].wait()
    dft(0)
    pl.semaphore_wait(barrier, NZ - 1 + NP - 1)
    z_start(0, 0, zs1[0], zr1[0])
    for j in range(1, nchunk):
        ld_air[j].wait()
        dft(j)
        if j == 1:
            z_start(0, 1, zs1[1], zr1[1])
    prepare()

    def step_a(j):
        z_wait(0, j, zs1[j], zr1[j])
        if j + 2 <= last:
            z_start(0, j + 2, zs1[j + 2], zr1[j + 2])
        perm1(j)
        p_start(1, j, ps1[j], mid[j])

    def step_b(j):
        p_wait(1, j, ps1[j], mid[j])
        middle(j)
        p_start(2, j, ret[j], pr2[j])

    def step_c(j):
        p_wait(2, j, pr2[j], pr2[j])
        perm2(j)
        z_start(3, j, zs2[j], fin[j])

    def step_d(j):
        z_wait(3, j, zs2[j], fin[j])
        if j == 0:
            ld_inv.wait()
        inverse(j)

    for i in range(nchunk + 3):
        if 0 <= i < nchunk:
            step_a(i)
        if 0 <= i - 1 < nchunk:
            step_b(i - 1)
        if 0 <= i - 2 < nchunk:
            step_c(i - 2)
        if 0 <= i - 3 < nchunk:
            step_d(i - 3)

    for j in range(nchunk):
        z_sent(0, j, zs1[j], zr1[j])
        p_sent(1, j, ps1[j])
        p_sent(2, j, pr2[j])
        z_sent(3, j, zs2[j], fin[j])
        pltpu.make_async_copy(airv[j], out_hbm.at[:, :, pl.ds(offs[j], CHUNKS[j])], out_sem.at[j]).wait()


def spectral(air, fwd, inv, pol, damp, warm, sea):
    bf = jnp.bfloat16
    n = len(CHUNKS)
    scratch = [
        pltpu.VMEM((N, N), bf), pltpu.VMEM((N, N), bf),
        pltpu.VMEM((2, LAT, LAT), bf), pltpu.VMEM((2, LAT, LAT), bf), pltpu.VMEM((2, LAT, LAT), bf),
        pltpu.VMEM((LAT, 768), jnp.float32), pltpu.VMEM((256, 256), bf), pltpu.VMEM((256, 256), bf),
    ]
    scratch += [pltpu.VMEM((2, N, w), bf) for w in CHUNKS]
    scratch += [pltpu.VMEM((NZ, 2, 128, w), bf) for w in CHUNKS]
    scratch += [pltpu.VMEM((NZ, 2, 128, w), bf) for w in CHUNKS]
    scratch += [pltpu.VMEM((NP, 2, 2, 16, w), bf) for w in CHUNKS]
    scratch += [pltpu.VMEM((2, 2, NP, 16, w), bf) for w in CHUNKS]
    scratch += [pltpu.VMEM((2, 2, NP, 16, w), bf) for w in CHUNKS]
    scratch += [pltpu.VMEM((NP, 2, 2, 16, w), bf) for w in CHUNKS]
    scratch += [pltpu.VMEM((NZ, 2, 128, w), bf) for w in CHUNKS]
    scratch += [pltpu.VMEM((NZ, 2, 128, w), bf) for w in CHUNKS]
    dma = pltpu.SemaphoreType.DMA
    scratch += [dma((4 + n,)), dma((n,)), dma((4, n)), dma((4, n)), dma((4, n))]
    anys = pl.BlockSpec(memory_space=pl.ANY)
    vm = pl.BlockSpec(memory_space=pltpu.VMEM)
    return pl.pallas_call(
        spectral_kernel,
        out_shape=jax.ShapeDtypeStruct(air.shape, bf),
        in_specs=[anys] * 5 + [vm] * 2,
        out_specs=anys,
        scratch_shapes=scratch,
        compiler_params=pltpu.CompilerParams(
            collective_id=0, has_side_effects=True, vmem_limit_bytes=60 << 20
        ),
        name="spectral",
    )(air, fwd, inv, pol, damp, warm, sea)


def ocean_update(
    state,
    tile_flux,
    mask_tile,
    count_tile,
    kernel_coefficients,
    local_exchange_matrix,
    patch_average_matrix,
    water_kernel_offset,
    water_readout_matrix,
):
    parallel_lines = mask_tile.shape[1]
    tile_width = mask_tile.shape[2]
    mask_f = mask_tile.astype(jnp.float32)
    masked = tile_flux * mask_tile[:, None].astype(jnp.bfloat16)
    fmean = (
        jnp.sum(masked.astype(jnp.float32), axis=(2, 3))
        / jnp.maximum(count_tile.astype(jnp.float32), 1.0)[:, None]
    )
    total = jnp.einsum(
        "fo,sfrw->sorw", local_exchange_matrix, masked, preferred_element_type=jnp.float32
    )
    for shift_row in range(3):
        for shift_col in range(3):
            window = state[
                :, :, shift_row : shift_row + parallel_lines, shift_col : shift_col + tile_width
            ]
            total = total + jnp.einsum(
                "io,sirw->sorw",
                kernel_coefficients[shift_row, shift_col],
                window,
                preferred_element_type=jnp.float32,
            )
    mean_term = jnp.sum(fmean[:, :, None] * patch_average_matrix[None], axis=1)
    total = total + mean_term[:, :, None, None] + water_kernel_offset[None, :, None, None]
    hidden = jax.nn.gelu(total, approximate=True).astype(jnp.bfloat16)
    update = jnp.einsum(
        "io,sirw->sorw", water_readout_matrix, hidden, preferred_element_type=jnp.float32
    )
    fresh = (
        state[:, :, 1 : 1 + parallel_lines, 1 : 1 + tile_width].astype(jnp.float32) + update
    ) * mask_f[:, None]
    return fresh.astype(jnp.bfloat16)


def shards(
    air_field_lattice,
    associated_polynomial_matrix,
    harmonic_damping_factor,
    boundary_exchange_projector,
    warmth_response_factor,
    water_patch_fields,
    kernel_coefficients,
    local_exchange_matrix,
    patch_average_matrix,
    water_kernel_offset,
    water_readout_matrix,
    patch_holder_index,
    water_point_indicator,
    water_point_totals,
):
    parallel_lines, meridian_number, channel_count = air_field_lattice.shape
    sec_count = lax.axis_size("sec")
    band_count = lax.axis_size("band")
    core_count = lax.axis_size("ch")
    slot_count = water_patch_fields.shape[0]
    flux_local = jnp.einsum(
        "anc,cf->fan",
        air_field_lattice,
        boundary_exchange_projector,
        preferred_element_type=jnp.float32,
    ).astype(jnp.bfloat16)
    gathered = lax.all_gather(flux_local, "band", axis=1, tiled=True)
    sec_id = lax.axis_index("sec")
    band_id = lax.axis_index("band")
    core_id = lax.axis_index("ch")
    owner_grid = patch_holder_index.reshape(sec_count, band_count, core_count, -1)
    tiles_per_row = owner_grid.shape[3]
    owner_group = lax.dynamic_index_in_dim(owner_grid, sec_id, 0, keepdims=False)
    owner_group = lax.dynamic_index_in_dim(owner_group, core_id, 1, keepdims=False)
    owner_flat = owner_group.reshape(-1)
    holders = jnp.arange(band_count, dtype=jnp.int32)
    mine_all = owner_flat[None, :] == holders[:, None]
    rank_all = jnp.cumsum(mine_all.astype(jnp.int32), axis=1) - 1
    slot_index = jnp.arange(slot_count, dtype=jnp.int32)
    pick_all = mine_all[:, None, :] & (rank_all[:, None, :] == slot_index[None, :, None])
    my_pick = lax.dynamic_index_in_dim(pick_all, band_id, 0, keepdims=False)
    flux_count = gathered.shape[0]
    tile_width = meridian_number // tiles_per_row
    pieces = gathered.reshape(flux_count, band_count, parallel_lines, tiles_per_row, tile_width)
    chooser = my_pick.reshape(slot_count, band_count, tiles_per_row).astype(jnp.bfloat16)
    tile_flux = jnp.einsum(
        "sbj,fbrjw->sfrw", chooser, pieces, preferred_element_type=jnp.float32
    ).astype(jnp.bfloat16)
    ocean_next = ocean_update(
        water_patch_fields,
        tile_flux,
        water_point_indicator,
        water_point_totals,
        kernel_coefficients,
        local_exchange_matrix,
        patch_average_matrix,
        water_kernel_offset,
        water_readout_matrix,
    )
    sea_slots = ocean_next[:, 0]
    sea_all = lax.all_gather(sea_slots, "band", axis=0, tiled=True)
    rank_tile = jnp.sum(jnp.where(mine_all, rank_all, 0), axis=0)
    my_owners = lax.dynamic_index_in_dim(owner_group, band_id, 0, keepdims=False)
    my_ranks = lax.dynamic_slice_in_dim(rank_tile, band_id * tiles_per_row, tiles_per_row)
    target = my_owners * slot_count + my_ranks
    selector = (
        target[:, None] == jnp.arange(band_count * slot_count, dtype=jnp.int32)[None, :]
    ).astype(jnp.bfloat16)
    water_patches = jnp.einsum(
        "jk,krw->rjw", selector, sea_all, preferred_element_type=jnp.float32
    ).astype(jnp.bfloat16)
    water_skin_warmth = water_patches.reshape(parallel_lines, meridian_number)
    fwd, inv = basis_tables()
    advanced = spectral(
        air_field_lattice,
        fwd,
        inv,
        associated_polynomial_matrix,
        harmonic_damping_factor,
        warmth_response_factor[None, :],
        water_skin_warmth.astype(jnp.float32)[:, :, None],
    )
    return (advanced, ocean_next)


def solution(mesh):
    placed = (
        P(("sec", "band", "ch"), None, None),
        P(("sec", "band", "ch"), None, None),
        P(),
        P(),
        P(),
        P(("sec", "band", "ch"), None, None, None),
        P(),
        P(),
        P(),
        P(),
        P(),
        P(),
        P(("sec", "band", "ch"), None, None),
        P(("sec", "band", "ch")),
    )
    return jax.shard_map(
        shards,
        mesh=mesh,
        in_specs=placed,
        out_specs=(
            P(("sec", "band", "ch"), None, None),
            P(("sec", "band", "ch"), None, None, None),
        ),
        check_vma=False,
    )
```

```python
import functools
import math

import jax
import jax.numpy as jnp
import numpy as np
from jax import lax
from jax.experimental import pallas as pl
from jax.experimental.pallas import tpu as pltpu
from jax.sharding import PartitionSpec as P

MESH = pl.DeviceIdType.MESH
CHUNKS = (256, 256, 256)
NZ, NY, NX, NC = 8, 4, 4, 2
NP = NY * NX * NC
N = 1024
LAT = 512


def trig(a, b):
    phase = (a[:, None].astype(np.int64) * b[None, :]) % N
    angle = phase.astype(np.float64) * (2.0 * math.pi / N)
    return np.cos(angle).astype(np.float32), np.sin(angle).astype(np.float32)


def basis_tables():
    n = np.arange(N)
    zh, zl, part, y = np.meshgrid(np.arange(2), np.arange(4), np.arange(2), np.arange(4), indexing="ij")
    k_hi = (zl * 128 + y * 32 + zh * 16).reshape(-1)
    part_hi = part.reshape(-1)[:, None]
    k_lo = np.arange(16)
    ch, sh = trig(k_hi, n)
    cl, sl = trig(k_lo, n)
    u1 = np.where(part_hi == 0, ch, -sh)
    u2 = np.where(part_hi == 0, -sh, -ch)
    fwd = jnp.asarray(u1)[:, None, :] * jnp.asarray(cl)[None] + jnp.asarray(u2)[:, None, :] * jnp.asarray(sl)[None]
    fwd = fwd.astype(jnp.bfloat16).reshape(N, N)
    k_all = (k_hi[:, None] + k_lo[None, :]).reshape(-1)
    part_all = np.repeat(part.reshape(-1), 16)[None, :]
    c1, s1 = trig(np.arange(32) * 32, k_all)
    c0, s0 = trig(np.arange(32), k_all)
    v1 = np.where(part_all == 0, c1, -s1)
    v2 = np.where(part_all == 0, -s1, -c1)
    inv = jnp.asarray(v1)[:, None, :] * jnp.asarray(c0)[None] + jnp.asarray(v2)[:, None, :] * jnp.asarray(s0)[None]
    inv = inv.astype(jnp.bfloat16).reshape(N, N)
    return fwd, inv


def one_hot(rows, cols, fn):
    r = lax.broadcasted_iota(jnp.int32, (rows, cols), 0)
    c = lax.broadcasted_iota(jnp.int32, (rows, cols), 1)
    return jnp.where(fn(r, c), 1.0, 0.0).astype(jnp.bfloat16)


def true_lat(i):
    t = i & 1
    z_lo = (i >> 1) & 3
    z_hi = (i >> 3) & 1
    c = (i >> 4) & 1
    x = (i >> 5) & 3
    y = (i >> 7) & 3
    return (z_lo * 64 + y * 16 + z_hi * 8 + x * 2 + c) * 2 + t


def spectral_kernel(
    air_hbm, fwd_hbm, inv_hbm, pol_hbm, damp_hbm, patch_hbm, warm_ref, proj_ref, conv_ref,
    local_ref, mean_ref, bias_ref, read_ref, wet_ref, total_ref, slot_ref, owner_ref, rank_ref,
    out_hbm, ocean_hbm, *scr
):
    nchunk = len(CHUNKS)
    it = iter(scr)
    fwd, inv, pol, polp, polt, damp, q1, q2 = (next(it) for _ in range(8))
    airv = [next(it) for _ in CHUNKS]
    zs1 = [next(it) for _ in CHUNKS]
    zr1 = [next(it) for _ in CHUNKS]
    ps1 = [next(it) for _ in CHUNKS]
    mid = [next(it) for _ in CHUNKS]
    ret = [next(it) for _ in CHUNKS]
    pr2 = [next(it) for _ in CHUNKS]
    zs2 = [next(it) for _ in CHUNKS]
    fin = [next(it) for _ in CHUNKS]
    patch, x3, q3, q4, fpair, fall, spair, sall, seab, ocean = (next(it) for _ in range(10))
    load_sem, out_sem, send_sem, recv_sem, self_sem, xs_sem = (next(it) for _ in range(6))

    s = lax.axis_index("sec")
    b = lax.axis_index("band")
    c = lax.axis_index("ch")
    y = b // 8
    z_hi = lax.rem(b // 4, 2)
    x = lax.rem(b, 4)
    z = z_hi * 4 + s
    p = y * 8 + x * 2 + c
    yx = y * 4 + x

    def z_dev(zz):
        return (lax.rem(zz, 4), y * 8 + (zz // 4) * 4 + x, c)

    def p_dev(pp):
        return (s, (pp // 8) * 8 + z_hi * 4 + lax.rem(pp // 2, 4), lax.rem(pp, 2))

    offs = [0]
    for w in CHUNKS:
        offs.append(offs[-1] + w)

    loads = []

    def load(src, dst):
        copy = pltpu.make_async_copy(src, dst, load_sem.at[len(loads)])
        copy.start()
        loads.append(copy)
        return copy

    ld_fwd = load(fwd_hbm, fwd)
    ld_air = [load(air_hbm.at[:, :, pl.ds(offs[j], CHUNKS[j])], airv[j]) for j in range(nchunk)]
    ld_pol = load(pol_hbm, pol)
    ld_damp = load(damp_hbm, damp)
    ld_inv = load(inv_hbm, inv)
    ld_patch = load(patch_hbm, patch)

    barrier = pltpu.get_barrier_semaphore()

    def greet_z(i, _):
        pl.semaphore_signal(barrier, inc=1, device_id=z_dev(lax.rem(z + i, NZ)), device_id_type=MESH)
        return 0

    def greet_p(i, _):
        pl.semaphore_signal(barrier, inc=1, device_id=p_dev(lax.rem(p + i, NP)), device_id_type=MESH)
        return 0

    lax.fori_loop(1, NZ, greet_z, 0)
    lax.fori_loop(1, NP, greet_p, 0)

    def z_copy(stage, j, src, dst, i):
        to = lax.rem(z + i, NZ)
        return pltpu.make_async_remote_copy(
            src_ref=src.at[to], dst_ref=dst.at[z],
            send_sem=send_sem.at[stage, j], recv_sem=recv_sem.at[stage, j],
            device_id=z_dev(to), device_id_type=MESH,
        )

    def z_start(stage, j, src, dst):
        pltpu.make_async_copy(src.at[z], dst.at[z], self_sem.at[stage, j]).start()

        def go(i, _):
            z_copy(stage, j, src, dst, i).start()
            return 0

        lax.fori_loop(1, NZ, go, 0)

    def z_wait(stage, j, src, dst):
        pltpu.make_async_copy(src.at[z], dst.at[z], self_sem.at[stage, j]).wait()
        pltpu.make_async_copy(src.at[pl.ds(0, NZ - 1)], dst.at[pl.ds(0, NZ - 1)], recv_sem.at[stage, j]).wait()

    def z_sent(stage, j, src, dst):
        pltpu.make_async_copy(src.at[pl.ds(0, NZ - 1)], dst.at[pl.ds(0, NZ - 1)], send_sem.at[stage, j]).wait()

    def p_start(stage, j, src, dst):
        def pick(to):
            if stage == 1:
                return src.at[to], dst.at[:, :, p]
            return src.at[:, :, to], dst.at[p]

        a, d = pick(p)
        pltpu.make_async_copy(a, d, self_sem.at[stage, j]).start()

        def go(i, _):
            to = lax.rem(p + i, NP)
            a, d = pick(to)
            pltpu.make_async_remote_copy(
                src_ref=a, dst_ref=d, send_sem=send_sem.at[stage, j], recv_sem=recv_sem.at[stage, j],
                device_id=p_dev(to), device_id_type=MESH,
            ).start()
            return 0

        lax.fori_loop(1, NP, go, 0)

    def p_wait(stage, j, flat, whole):
        a = flat.at[0]
        pltpu.make_async_copy(a, a, self_sem.at[stage, j]).wait()
        a = flat.at[pl.ds(0, NP - 1)]
        pltpu.make_async_copy(a, a, recv_sem.at[stage, j]).wait()

    def p_sent(stage, j, flat):
        a = flat.at[pl.ds(0, NP - 1)]
        pltpu.make_async_copy(a, a, send_sem.at[stage, j]).wait()

    def dot(a, bb):
        return jnp.dot(a, bb, preferred_element_type=jnp.float32)

    def flip_copy(stage, buf):
        return pltpu.make_async_remote_copy(
            src_ref=buf.at[z_hi], dst_ref=buf.at[z_hi], send_sem=xs_sem.at[stage, 0], recv_sem=xs_sem.at[stage, 1],
            device_id=z_dev(lax.rem(z + 4, NZ)), device_id_type=MESH,
        )

    def spread_start(stage, pair, whole):
        pltpu.make_async_copy(pair, whole.at[yx], xs_sem.at[stage, 2]).start()

        def go(i, _):
            to = lax.rem(yx + i, 16)
            pltpu.make_async_remote_copy(
                src_ref=pair, dst_ref=whole.at[yx], send_sem=xs_sem.at[stage, 3], recv_sem=xs_sem.at[stage, 4],
                device_id=p_dev(to * 2 + c), device_id_type=MESH,
            ).start()
            return 0

        lax.fori_loop(1, 16, go, 0)

    def spread_wait(stage, pair, whole):
        pltpu.make_async_copy(pair, whole.at[yx], xs_sem.at[stage, 2]).wait()
        a = whole.at[pl.ds(0, 15)]
        pltpu.make_async_copy(a, a, xs_sem.at[stage, 4]).wait()

    def spread_sent(stage, whole):
        a = whole.at[pl.ds(0, 15)]
        pltpu.make_async_copy(a, a, xs_sem.at[stage, 3]).wait()

    def dot_t(a, bb):
        return lax.dot_general(a, bb, (((1,), (1,)), ((), ())), preferred_element_type=jnp.float32)

    def surface_flux():
        for j in range(nchunk):
            ld_air[j].wait() if j else None
        for t in range(2):
            acc = None
            for j in range(nchunk):
                part = dot_t(proj_ref[:, offs[j]:offs[j] + CHUNKS[j]], airv[j][t])
                acc = part if acc is None else acc + part
            acc = acc.astype(jnp.bfloat16)
            for q in range(4):
                fpair[z_hi, q, t] = acc[:, q * 256:(q + 1) * 256]

    def rows_first(i, _):
        for blk in range(4):
            rows = patch[i, blk * 256:(blk + 1) * 256, :]
            x3[i, :, blk * 64:(blk + 1) * 64, :] = dot(q3[...], rows).reshape(4, 64, 128)
        x3[i, :, 256:264, :] = dot(q4[...], patch[i, 776:1032, :]).reshape(4, 8, 128)
        return 0

    def ocean_step(i, sea):
        tile = slot_ref[i]
        owner_b = tile >> 2
        flux = fall[((owner_b >> 3) << 2) + (owner_b & 3), (owner_b >> 2) & 1, tile & 3].astype(jnp.float32)
        wet = wet_ref[i].astype(jnp.float32)
        masked = [flux[r] * wet[r:r + 1, :] for r in range(2)]
        whole = jnp.sum(masked[0] + masked[1], axis=1, keepdims=True)
        fmean = whole / jnp.maximum(total_ref[i].astype(jnp.float32), 1.0)
        shift = bias_ref[...]
        for f in range(8):
            shift = shift + mean_ref[:, f:f + 1] * fmean[f:f + 1, :]
        for r in range(2):
            wins = [
                x3[i, r + dr, dw:dw + 256, :].astype(jnp.bfloat16) for dr in range(3) for dw in range(3)
            ]
            pre = dot_t(conv_ref[...], jnp.concatenate(wins, axis=1))
            pre = pre + dot(local_ref[...], masked[r].astype(jnp.bfloat16)) + shift
            hidden = jax.nn.gelu(pre, approximate=True).astype(jnp.bfloat16)
            old = dot_t(read_ref[1], wins[4])
            new = (old + dot(read_ref[0], hidden)) * wet[r:r + 1, :]
            ocean[i, r] = new.astype(jnp.bfloat16)
            line = lax.broadcasted_iota(jnp.int32, (16, 256), 0)
            sea = jnp.where(line == 2 * i + r, jnp.broadcast_to(new[0:1, :], (16, 256)), sea)
        return sea

    def ocean_all():
        q3[...] = one_hot(256, 256, lambda r, q: ((r >> 6) == (q & 3)) & ((r & 63) == (q >> 2)))
        q4[...] = one_hot(32, 256, lambda r, q: q == (r & 7) * 4 + (r >> 3) + 248)
        ld_patch.wait()
        lax.fori_loop(0, 6, rows_first, 0)
        spread_wait(0, fpair, fall)
        sea = lax.fori_loop(0, 6, ocean_step, jnp.zeros((16, 256), jnp.float32))
        spair[z_hi] = sea.astype(jnp.bfloat16)
        flip_copy(1, spair).start()
        pltpu.make_async_copy(ocean, ocean_hbm, xs_sem.at[0, 5]).start()

    def place_sea():
        spread_wait(1, spair, sall)
        for q in range(4):
            at = (lax.axis_index("band")) * 4 + q
            owner = owner_ref[at]
            slot = rank_ref[at]
            tile = sall[((owner >> 3) << 2) + (owner & 3), (owner >> 2) & 1].astype(jnp.float32)
            for t in range(2):
                line = lax.broadcasted_iota(jnp.int32, (16, 256), 0)
                row = jnp.sum(jnp.where(line == 2 * slot + t, tile, 0.0), axis=0, keepdims=True)
                seab[t, q * 256:(q + 1) * 256, :] = jnp.broadcast_to(row, (128, 256)).T

    def dft(j):
        w = CHUNKS[j]

        def body(i, _):
            t = i // 4
            m = lax.rem(i, 4)
            rows = fwd[pl.ds(pl.multiple_of(m * 256, 256), 256), :]
            f = dot(rows, airv[j][t]).astype(jnp.bfloat16)
            zs1[j][pl.ds(m * 2, 2), t] = f.reshape(2, 128, w)
            return 0

        lax.fori_loop(0, 8, body, 0)

    def perm1(j):
        w = CHUNKS[j]

        def body(i, _):
            part = i // 4
            g = lax.rem(i, 4)
            r0 = pl.multiple_of(part * 64 + g * 16, 16)
            xin = zr1[j][:, :, pl.ds(r0, 16), :].reshape(256, w)
            yo = dot(q1[...], xin).astype(jnp.bfloat16)
            ps1[j][pl.ds(g * 8, 8), part] = yo.reshape(8, 2, 16, w)
            return 0

        lax.fori_loop(0, 8, body, 0)

    def middle(j):
        w = CHUNKS[j]
        d0 = offs[j]

        def body(i, _):
            part = i // 2
            k = lax.rem(i, 2)
            xin = mid[j][part, k].reshape(LAT, w)
            sp = dot(polp[k], xin)
            sc = (sp * damp[:, d0:d0 + w]).astype(jnp.bfloat16)
            fo = dot(polt[k], sc).astype(jnp.bfloat16)
            ret[j][part, k] = fo.reshape(NP, 16, w)
            return 0

        lax.fori_loop(0, 4, body, 0)

    def perm2(j):
        w = CHUNKS[j]

        def body(i, _):
            part = i // 4
            g = lax.rem(i, 4)
            r0 = pl.multiple_of(part * 64 + g * 16, 16)
            xin = pr2[j][pl.ds(g * 8, 8), part].reshape(256, w)
            yo = dot(q2[...], xin).astype(jnp.bfloat16)
            zs2[j][:, :, pl.ds(r0, 16), :] = yo.reshape(8, 2, 16, w)
            return 0

        lax.fori_loop(0, 8, body, 0)

    def inverse(j):
        w = CHUNKS[j]
        d0 = offs[j]

        def body(i, _):
            t = i // 4
            m = pl.multiple_of(lax.rem(i, 4) * 256, 256)
            rows = inv[pl.ds(m, 256), :]
            rec = dot(rows, fin[j][:, t].reshape(N, w)) * (1.0 / 512.0)
            old = airv[j][t, pl.ds(m, 256), :].astype(jnp.float32)
            sea = seab[t, pl.ds(m, 256), :]
            sea = jnp.concatenate([sea] * (w // 128), axis=1)
            new = old + rec + sea * warm_ref[:, d0:d0 + w]
            airv[j][t, pl.ds(m, 256), :] = new.astype(jnp.bfloat16)
            return 0

        lax.fori_loop(0, 8, body, 0)
        pltpu.make_async_copy(airv[j], out_hbm.at[:, :, pl.ds(d0, w)], out_sem.at[j]).start()

    def prepare():
        q1[...] = one_hot(256, 256, lambda r, q: (((r & 15) == (q >> 4)) & ((r >> 5) == ((q >> 1) & 7)) & (((r >> 4) & 1) == (q & 1))))
        q2[...] = one_hot(256, 256, lambda q, r: (((r & 15) == (q >> 4)) & ((r >> 5) == ((q >> 1) & 7)) & (((r >> 4) & 1) == (q & 1))))
        ld_pol.wait()
        sel = one_hot(LAT, LAT, lambda r, q: r == true_lat(q))
        selt = one_hot(LAT, LAT, lambda r, q: true_lat(r) == q)
        for k in range(2):
            polp[k] = dot(pol[k], sel).astype(jnp.bfloat16)
            polt[k] = lax.dot_general(
                selt, pol[k], (((1,), (1,)), ((), ())), preferred_element_type=jnp.float32
            ).astype(jnp.bfloat16)
        ld_damp.wait()

    last = nchunk - 1
    ld_fwd.wait()
    ld_air[0].wait()
    dft(0)
    pl.semaphore_wait(barrier, NZ - 1 + NP - 1)
    z_start(0, 0, zs1[0], zr1[0])
    surface_flux()
    flip_copy(0, fpair).start()
    for j in range(1, nchunk):
        dft(j)
        if j == 1:
            z_start(0, 1, zs1[1], zr1[1])
    prepare()
    flip_copy(0, fpair).wait()
    spread_start(0, fpair, fall)

    def step_a(j):
        z_wait(0, j, zs1[j], zr1[j])
        if j + 2 <= last:
            z_start(0, j + 2, zs1[j + 2], zr1[j + 2])
        perm1(j)
        p_start(1, j, ps1[j], mid[j])

    def step_b(j):
        p_wait(1, j, ps1[j], mid[j])
        middle(j)
        p_start(2, j, ret[j], pr2[j])

    def step_c(j):
        p_wait(2, j, pr2[j], pr2[j])
        perm2(j)
        z_start(3, j, zs2[j], fin[j])

    def step_d(j):
        z_wait(3, j, zs2[j], fin[j])
        if j == 0:
            ld_inv.wait()
        inverse(j)

    for i in range(nchunk + 3):
        if 0 <= i < nchunk:
            step_a(i)
        if i == 0:
            ocean_all()
        if i == 1:
            flip_copy(1, spair).wait()
            spread_start(1, spair, sall)
        if i == 3:
            place_sea()
        if 0 <= i - 1 < nchunk:
            step_b(i - 1)
        if 0 <= i - 2 < nchunk:
            step_c(i - 2)
        if 0 <= i - 3 < nchunk:
            step_d(i - 3)

    spread_sent(0, fall)
    spread_sent(1, sall)
    pltpu.make_async_copy(ocean, ocean_hbm, xs_sem.at[0, 5]).wait()
    for j in range(nchunk):
        z_sent(0, j, zs1[j], zr1[j])
        p_sent(1, j, ps1[j])
        p_sent(2, j, pr2[j])
        z_sent(3, j, zs2[j], fin[j])
        pltpu.make_async_copy(airv[j], out_hbm.at[:, :, pl.ds(offs[j], CHUNKS[j])], out_sem.at[j]).wait()


def spectral(air, fwd, inv, pol, damp, patch, *rest):
    bf = jnp.bfloat16
    n = len(CHUNKS)
    scratch = [
        pltpu.VMEM((N, N), bf), pltpu.VMEM((N, N), bf),
        pltpu.VMEM((2, LAT, LAT), bf), pltpu.VMEM((2, LAT, LAT), bf), pltpu.VMEM((2, LAT, LAT), bf),
        pltpu.VMEM((LAT, 768), jnp.float32), pltpu.VMEM((256, 256), bf), pltpu.VMEM((256, 256), bf),
    ]
    scratch += [pltpu.VMEM((2, N, w), bf) for w in CHUNKS]
    scratch += [pltpu.VMEM((NZ, 2, 128, w), bf) for w in CHUNKS]
    scratch += [pltpu.VMEM((NZ, 2, 128, w), bf) for w in CHUNKS]
    scratch += [pltpu.VMEM((NP, 2, 2, 16, w), bf) for w in CHUNKS]
    scratch += [pltpu.VMEM((2, 2, NP, 16, w), bf) for w in CHUNKS]
    scratch += [pltpu.VMEM((2, 2, NP, 16, w), bf) for w in CHUNKS]
    scratch += [pltpu.VMEM((NP, 2, 2, 16, w), bf) for w in CHUNKS]
    scratch += [pltpu.VMEM((NZ, 2, 128, w), bf) for w in CHUNKS]
    scratch += [pltpu.VMEM((NZ, 2, 128, w), bf) for w in CHUNKS]
    scratch += [
        pltpu.VMEM((6, 1032, 128), bf), pltpu.VMEM((6, 4, 264, 128), jnp.float32),
        pltpu.VMEM((256, 256), bf), pltpu.VMEM((32, 256), bf),
        pltpu.VMEM((2, 4, 2, 8, 256), bf), pltpu.VMEM((16, 2, 4, 2, 8, 256), bf),
        pltpu.VMEM((2, 16, 256), bf), pltpu.VMEM((16, 2, 16, 256), bf),
        pltpu.VMEM((2, N, 128), jnp.float32), pltpu.VMEM((6, 2, 128, 256), bf),
    ]
    dma = pltpu.SemaphoreType.DMA
    scratch += [dma((5 + n,)), dma((n,)), dma((4, n)), dma((4, n)), dma((4, n)), dma((2, 6))]
    anys = pl.BlockSpec(memory_space=pl.ANY)
    vm = pl.BlockSpec(memory_space=pltpu.VMEM)
    sm = pl.BlockSpec(memory_space=pltpu.SMEM)
    return pl.pallas_call(
        spectral_kernel,
        out_shape=(jax.ShapeDtypeStruct(air.shape, bf), jax.ShapeDtypeStruct((6, 2, 128, 256), bf)),
        in_specs=[anys] * 6 + [vm] * 8 + [sm] * 4,
        out_specs=(anys, anys),
        scratch_shapes=scratch,
        compiler_params=pltpu.CompilerParams(
            collective_id=0, has_side_effects=True, vmem_limit_bytes=60 << 20
        ),
        name="spectral",
    )(air, fwd, inv, pol, damp, patch, *rest)


def shards(
    air_field_lattice,
    associated_polynomial_matrix,
    harmonic_damping_factor,
    boundary_exchange_projector,
    warmth_response_factor,
    water_patch_fields,
    kernel_coefficients,
    local_exchange_matrix,
    patch_average_matrix,
    water_kernel_offset,
    water_readout_matrix,
    patch_holder_index,
    water_point_indicator,
    water_point_totals,
):
    sec_id = lax.axis_index("sec")
    band_id = lax.axis_index("band")
    core_id = lax.axis_index("ch")
    owner_grid = patch_holder_index.reshape(4, 32, 2, 4)
    owners = lax.dynamic_slice(owner_grid, (sec_id, 0, core_id, 0), (1, 32, 1, 4)).reshape(128)
    at = jnp.arange(128, dtype=jnp.int32)
    same = owners[:, None] == owners[None, :]
    ranks = jnp.sum((same & (at[None, :] < at[:, None])).astype(jnp.int32), axis=1)
    slot = jnp.arange(6, dtype=jnp.int32)
    chosen = (owners[None, :] == band_id) & (ranks[None, :] == slot[:, None])
    slot_tile = jnp.sum(jnp.where(chosen, at[None, :], 0), axis=1)
    fwd, inv = basis_tables()
    bf = jnp.bfloat16
    conv = kernel_coefficients.reshape(9 * 128, 128).T
    readout = jnp.stack([water_readout_matrix.T, jnp.eye(128, dtype=bf)])
    patches = water_patch_fields.transpose(0, 3, 2, 1).reshape(6, 1032, 128)
    advanced, ocean = spectral(
        air_field_lattice,
        fwd,
        inv,
        associated_polynomial_matrix,
        harmonic_damping_factor,
        patches,
        warmth_response_factor[None, :],
        boundary_exchange_projector.T,
        conv,
        local_exchange_matrix.T,
        patch_average_matrix.T,
        water_kernel_offset[:, None],
        readout,
        water_point_indicator,
        water_point_totals,
        slot_tile,
        owners,
        ranks,
    )
    return (advanced, ocean.transpose(0, 2, 1, 3))


def solution(mesh):
    placed = (
        P(("sec", "band", "ch"), None, None),
        P(("sec", "band", "ch"), None, None),
        P(),
        P(),
        P(),
        P(("sec", "band", "ch"), None, None, None),
        P(),
        P(),
        P(),
        P(),
        P(),
        P(),
        P(("sec", "band", "ch"), None, None),
        P(("sec", "band", "ch")),
    )
    return jax.shard_map(
        shards,
        mesh=mesh,
        in_specs=placed,
        out_specs=(
            P(("sec", "band", "ch"), None, None),
            P(("sec", "band", "ch"), None, None, None),
        ),
        check_vma=False,
    )
```

```python
import functools
import math

import jax
import jax.numpy as jnp
import numpy as np
from jax import lax
from jax.experimental import pallas as pl
from jax.experimental.pallas import tpu as pltpu
from jax.sharding import PartitionSpec as P

MESH = pl.DeviceIdType.MESH
CHUNKS = (128,) * 6
WINDOW = 3
NZ, NY, NX, NC = 8, 4, 4, 2
NP = NY * NX * NC
N = 1024
LAT = 512


def basis_table():
    z_hi, z_lo, part, y, low = np.meshgrid(
        np.arange(2), np.arange(4), np.arange(2), np.arange(4), np.arange(16), indexing="ij"
    )
    k = (z_lo * 128 + y * 32 + z_hi * 16 + low).reshape(-1)[:, None]
    angle = ((k * np.arange(N)[None, :]) % N).astype(np.float64) * (2.0 * math.pi / N)
    table = np.where(part.reshape(-1)[:, None] == 0, np.cos(angle), -np.sin(angle))
    return table.astype(np.float32).astype(jnp.bfloat16)


def one_hot(rows, cols, fn):
    r = lax.broadcasted_iota(jnp.int32, (rows, cols), 0)
    c = lax.broadcasted_iota(jnp.int32, (rows, cols), 1)
    return jnp.where(fn(r, c), 1.0, 0.0).astype(jnp.bfloat16)


def true_lat(i):
    t = i & 1
    z_lo = (i >> 1) & 3
    z_hi = (i >> 3) & 1
    c = (i >> 4) & 1
    x = (i >> 5) & 3
    y = (i >> 7) & 3
    return (z_lo * 64 + y * 16 + z_hi * 8 + x * 2 + c) * 2 + t


def spectral_kernel(
    air_hbm, fwd_hbm, pol_hbm, damp_hbm, patch_hbm, warm_ref, proj_ref, conv_ref,
    local_ref, mean_ref, bias_ref, read_ref, wet_ref, total_ref, owner_ref,
    out_hbm, ocean_hbm, *scr
):
    nchunk = len(CHUNKS)
    it = iter(scr)
    fwd, inv, pol, polp, polt, damp, q1, q2 = (next(it) for _ in range(8))
    airv = [next(it) for _ in CHUNKS]
    zs1 = [next(it) for _ in CHUNKS]
    zr1 = [next(it) for _ in CHUNKS]
    ps1 = [next(it) for _ in CHUNKS]
    mid = [next(it) for _ in CHUNKS]
    ret = [next(it) for _ in CHUNKS]
    pr2 = [next(it) for _ in CHUNKS]
    zs2 = [next(it) for _ in CHUNKS]
    fin = [next(it) for _ in CHUNKS]
    patch, x3, q3, q4, fpair, fall, spair, sall, seab, ocean = (next(it) for _ in range(10))
    conv_t, read_t, local_t, eye, route = (next(it) for _ in range(5))
    load_sem, out_sem, send_sem, recv_sem, self_sem, xs_sem = (next(it) for _ in range(6))

    s = lax.axis_index("sec")
    b = lax.axis_index("band")
    c = lax.axis_index("ch")
    y = b // 8
    z_hi = lax.rem(b // 4, 2)
    x = lax.rem(b, 4)
    z = z_hi * 4 + s
    p = y * 8 + x * 2 + c
    yx = y * 4 + x

    def z_dev(zz):
        return (lax.rem(zz, 4), y * 8 + (zz // 4) * 4 + x, c)

    def p_dev(pp):
        return (s, (pp // 8) * 8 + z_hi * 4 + lax.rem(pp // 2, 4), lax.rem(pp, 2))

    offs = [0]
    for w in CHUNKS:
        offs.append(offs[-1] + w)

    loads = []

    def load(src, dst):
        copy = pltpu.make_async_copy(src, dst, load_sem.at[len(loads)])
        copy.start()
        loads.append(copy)
        return copy

    ld_fwd = load(fwd_hbm, fwd)
    ld_air = [load(air_hbm.at[:, :, pl.ds(offs[j], CHUNKS[j])], airv[j]) for j in range(nchunk)]
    ld_pol = load(pol_hbm, pol)
    ld_damp = load(damp_hbm, damp)
    ld_patch = load(patch_hbm, patch)

    barrier = pltpu.get_barrier_semaphore()

    def greet_z(i, _):
        pl.semaphore_signal(barrier, inc=1, device_id=z_dev(lax.rem(z + i, NZ)), device_id_type=MESH)
        return 0

    def greet_p(i, _):
        pl.semaphore_signal(barrier, inc=1, device_id=p_dev(lax.rem(p + i, NP)), device_id_type=MESH)
        return 0

    lax.fori_loop(1, NZ, greet_z, 0)
    lax.fori_loop(1, NP, greet_p, 0)

    def z_copy(stage, j, src, dst, i):
        near = (i + 1) // 2
        to = lax.rem(z + jnp.where(lax.rem(i, 2) == 1, near, NZ - near), NZ)
        return pltpu.make_async_remote_copy(
            src_ref=src.at[to], dst_ref=dst.at[z],
            send_sem=send_sem.at[stage, j], recv_sem=recv_sem.at[stage, j],
            device_id=z_dev(to), device_id_type=MESH,
        )

    def z_start(stage, j, src, dst):
        pltpu.make_async_copy(src.at[z], dst.at[z], self_sem.at[stage, j]).start()

        def go(i, _):
            z_copy(stage, j, src, dst, i).start()
            return 0

        lax.fori_loop(1, NZ, go, 0)

    def z_wait(stage, j, src, dst):
        pltpu.make_async_copy(src.at[z], dst.at[z], self_sem.at[stage, j]).wait()
        pltpu.make_async_copy(src.at[pl.ds(0, NZ - 1)], dst.at[pl.ds(0, NZ - 1)], recv_sem.at[stage, j]).wait()

    def z_sent(stage, j, src, dst):
        pltpu.make_async_copy(src.at[pl.ds(0, NZ - 1)], dst.at[pl.ds(0, NZ - 1)], send_sem.at[stage, j]).wait()

    def p_start(stage, j, src, dst):
        def pick(to):
            if stage == 1:
                return src.at[to], dst.at[:, :, p]
            return src.at[:, :, to], dst.at[p]

        a, d = pick(p)
        pltpu.make_async_copy(a, d, self_sem.at[stage, j]).start()

        def go(i, _):
            to = lax.rem(p + i, NP)
            a, d = pick(to)
            pltpu.make_async_remote_copy(
                src_ref=a, dst_ref=d, send_sem=send_sem.at[stage, j], recv_sem=recv_sem.at[stage, j],
                device_id=p_dev(to), device_id_type=MESH,
            ).start()
            return 0

        lax.fori_loop(1, NP, go, 0)

    def p_wait(stage, j, flat, whole):
        a = flat.at[0]
        pltpu.make_async_copy(a, a, self_sem.at[stage, j]).wait()
        a = flat.at[pl.ds(0, NP - 1)]
        pltpu.make_async_copy(a, a, recv_sem.at[stage, j]).wait()

    def p_sent(stage, j, flat):
        a = flat.at[pl.ds(0, NP - 1)]
        pltpu.make_async_copy(a, a, send_sem.at[stage, j]).wait()

    def dot(a, bb):
        return jnp.dot(a, bb, preferred_element_type=jnp.float32)

    def flip_copy(stage, buf):
        return pltpu.make_async_remote_copy(
            src_ref=buf.at[z_hi], dst_ref=buf.at[z_hi], send_sem=xs_sem.at[stage, 0], recv_sem=xs_sem.at[stage, 1],
            device_id=z_dev(lax.rem(z + 4, NZ)), device_id_type=MESH,
        )

    def spread_start(stage, pair, whole):
        pltpu.make_async_copy(pair, whole.at[yx], xs_sem.at[stage, 2]).start()

        def go(i, _):
            to = lax.rem(yx + i, 16)
            pltpu.make_async_remote_copy(
                src_ref=pair, dst_ref=whole.at[yx], send_sem=xs_sem.at[stage, 3], recv_sem=xs_sem.at[stage, 4],
                device_id=p_dev(to * 2 + c), device_id_type=MESH,
            ).start()
            return 0

        lax.fori_loop(1, 16, go, 0)

    def spread_wait(stage, pair, whole):
        pltpu.make_async_copy(pair, whole.at[yx], xs_sem.at[stage, 2]).wait()
        a = whole.at[pl.ds(0, 15)]
        pltpu.make_async_copy(a, a, xs_sem.at[stage, 4]).wait()

    def spread_sent(stage, whole):
        a = whole.at[pl.ds(0, 15)]
        pltpu.make_async_copy(a, a, xs_sem.at[stage, 3]).wait()

    def dot_t(a, bb):
        return lax.dot_general(a, bb, (((1,), (1,)), ((), ())), preferred_element_type=jnp.float32)

    def surface_flux():
        for j in range(nchunk):
            ld_air[j].wait() if j else None
        for t in range(2):
            acc = None
            for j in range(nchunk):
                part = dot_t(proj_ref[:, offs[j]:offs[j] + CHUNKS[j]], airv[j][t])
                acc = part if acc is None else acc + part
            acc = acc.astype(jnp.bfloat16)
            for q in range(4):
                fpair[z_hi, q, t] = acc[:, q * 256:(q + 1) * 256]

    def rows_first(i, _):
        for blk in range(4):
            rows = patch[i, blk * 256:(blk + 1) * 256, :]
            x3[i, :, blk * 64:(blk + 1) * 64, :] = dot(q3[...], rows).reshape(4, 64, 128)
        x3[i, :, 256:264, :] = dot(q4[...], patch[i, 776:1032, :]).reshape(4, 8, 128)
        return 0

    def ocean_step(i, sea):
        tile = route[i]
        owner_b = tile >> 2
        flux = fall[((owner_b >> 3) << 2) + (owner_b & 3), (owner_b >> 2) & 1, tile & 3].astype(jnp.float32)
        wet = wet_ref[i].astype(jnp.float32)
        masked = [flux[r] * wet[r:r + 1, :] for r in range(2)]
        whole = jnp.sum(masked[0] + masked[1], axis=1, keepdims=True)
        fmean = whole / jnp.maximum(total_ref[i].astype(jnp.float32), 1.0)
        row = jnp.sum(mean_ref[...] * fmean, axis=0, keepdims=True) + bias_ref[...]
        shift = jnp.broadcast_to(row, (128, 128)).T
        shift = jnp.concatenate([shift, shift], axis=1)
        for r in range(2):
            wins = [
                x3[i, r + dr, dw:dw + 256, :].astype(jnp.bfloat16) for dr in range(3) for dw in range(3)
            ]
            pre = dot_t(conv_t[...], jnp.concatenate(wins, axis=1))
            pre = pre + dot(local_t[...], masked[r].astype(jnp.bfloat16)) + shift
            hidden = jax.nn.gelu(pre, approximate=True).astype(jnp.bfloat16)
            old = dot_t(eye[:128, :128], wins[4])
            new = (old + dot(read_t[...], hidden)) * wet[r:r + 1, :]
            ocean[i, r] = new.astype(jnp.bfloat16)
            line = lax.broadcasted_iota(jnp.int32, (16, 256), 0)
            sea = jnp.where(line == 2 * i + r, jnp.broadcast_to(new[0:1, :], (16, 256)), sea)
        return sea

    def ocean_prepare():
        q3[...] = one_hot(256, 256, lambda r, q: ((r >> 6) == (q & 3)) & ((r & 63) == (q >> 2)))
        q4[...] = one_hot(32, 256, lambda r, q: q == (r & 7) * 4 + (r >> 3) + 248)
        small = eye[:128, :128]
        conv_t[...] = dot_t(small, conv_ref[...]).astype(jnp.bfloat16)
        read_t[...] = dot_t(small, read_ref[...]).astype(jnp.bfloat16)
        local_t[...] = dot_t(small, local_ref[...]).astype(jnp.bfloat16)
        ld_patch.wait()
        lax.fori_loop(0, 6, rows_first, 0)

    def find_routes():
        mine = [owner_ref[q, (s * 32 + b) * 2 + c] for q in range(4)]

        def scan(i, held):
            held = list(held)
            for q in range(4):
                owner = owner_ref[q, (s * 32 + i) * 2 + c]
                hit = owner == b
                for k in range(6):
                    held[k] = jnp.where(hit & (held[6] == k), i * 4 + q, held[k])
                held[6] = held[6] + jnp.where(hit, 1, 0)
                for k in range(4):
                    before = i * 4 + q < b * 4 + k
                    held[7 + k] = held[7 + k] + jnp.where((owner == mine[k]) & before, 1, 0)
            return tuple(held)

        held = lax.fori_loop(0, 32, scan, tuple(jnp.int32(0) for _ in range(11)))
        for k in range(6):
            route[k] = held[k]
        for k in range(4):
            route[8 + k] = mine[k]
            route[12 + k] = held[7 + k]

    def ocean_all():
        spread_wait(0, fpair, fall)
        sea = lax.fori_loop(0, 6, ocean_step, jnp.zeros((16, 256), jnp.float32))
        spair[z_hi] = sea.astype(jnp.bfloat16)
        flip_copy(1, spair).start()
        pltpu.make_async_copy(ocean, ocean_hbm, xs_sem.at[0, 5]).start()

    def place_sea():
        spread_wait(1, spair, sall)
        for q in range(4):
            owner = route[8 + q]
            slot = route[12 + q]
            tile = sall[((owner >> 3) << 2) + (owner & 3), (owner >> 2) & 1].astype(jnp.float32)
            for t in range(2):
                line = lax.broadcasted_iota(jnp.int32, (16, 256), 0)
                row = jnp.sum(jnp.where(line == 2 * slot + t, tile, 0.0), axis=0, keepdims=True)
                seab[t, q * 256:(q + 1) * 256, :] = jnp.broadcast_to(row, (128, 256)).T

    def dft(j):
        w = CHUNKS[j]

        def body(i, _):
            t = i // 4
            m = lax.rem(i, 4)
            rows = fwd[pl.ds(pl.multiple_of(m * 256, 256), 256), :]
            f = dot(rows, airv[j][t]).astype(jnp.bfloat16)
            zs1[j][pl.ds(m * 2, 2), t] = f.reshape(2, 128, w)
            return 0

        lax.fori_loop(0, 8, body, 0)

    def perm1(j):
        w = CHUNKS[j]

        def body(i, _):
            part = i // 4
            g = lax.rem(i, 4)
            r0 = pl.multiple_of(part * 64 + g * 16, 16)
            xin = zr1[j][:, :, pl.ds(r0, 16), :].reshape(256, w)
            yo = dot(q1[...], xin).astype(jnp.bfloat16)
            ps1[j][pl.ds(g * 8, 8), part] = yo.reshape(8, 2, 16, w)
            return 0

        lax.fori_loop(0, 8, body, 0)

    def middle(j):
        w = CHUNKS[j]
        d0 = offs[j]

        def body(i, _):
            part = i // 2
            k = lax.rem(i, 2)
            xin = mid[j][part, k].reshape(LAT, w)
            sp = dot(polp[k], xin)
            sc = (sp * damp[:, d0:d0 + w]).astype(jnp.bfloat16)
            fo = dot(polt[k], sc).astype(jnp.bfloat16)
            ret[j][part, k] = fo.reshape(NP, 16, w)
            return 0

        lax.fori_loop(0, 4, body, 0)

    def perm2(j):
        w = CHUNKS[j]

        def body(i, _):
            part = i // 4
            g = lax.rem(i, 4)
            r0 = pl.multiple_of(part * 64 + g * 16, 16)
            xin = pr2[j][pl.ds(g * 8, 8), part].reshape(256, w)
            yo = dot(q2[...], xin).astype(jnp.bfloat16)
            zs2[j][:, :, pl.ds(r0, 16), :] = yo.reshape(8, 2, 16, w)
            return 0

        lax.fori_loop(0, 8, body, 0)

    def inverse(j):
        w = CHUNKS[j]
        d0 = offs[j]

        def body(i, _):
            t = i // 4
            m = pl.multiple_of(lax.rem(i, 4) * 256, 256)
            rows = inv[pl.ds(m, 256), :]
            rec = dot(rows, fin[j][:, t].reshape(N, w)) * (1.0 / 512.0)
            old = airv[j][t, pl.ds(m, 256), :].astype(jnp.float32)
            sea = seab[t, pl.ds(m, 256), :]
            sea = jnp.concatenate([sea] * (w // 128), axis=1)
            new = old + rec + sea * warm_ref[d0:d0 + w][None, :]
            airv[j][t, pl.ds(m, 256), :] = new.astype(jnp.bfloat16)
            return 0

        lax.fori_loop(0, 8, body, 0)
        pltpu.make_async_copy(airv[j], out_hbm.at[:, :, pl.ds(d0, w)], out_sem.at[j]).start()

    def prepare():
        q1[...] = one_hot(256, 256, lambda r, q: (((r & 15) == (q >> 4)) & ((r >> 5) == ((q >> 1) & 7)) & (((r >> 4) & 1) == (q & 1))))
        q2[...] = one_hot(256, 256, lambda q, r: (((r & 15) == (q >> 4)) & ((r >> 5) == ((q >> 1) & 7)) & (((r >> 4) & 1) == (q & 1))))
        ld_pol.wait()
        sel = one_hot(LAT, LAT, lambda r, q: r == true_lat(q))
        selt = one_hot(LAT, LAT, lambda r, q: true_lat(r) == q)
        for k in range(2):
            polp[k] = dot(pol[k], sel).astype(jnp.bfloat16)
            polt[k] = lax.dot_general(
                selt, pol[k], (((1,), (1,)), ((), ())), preferred_element_type=jnp.float32
            ).astype(jnp.bfloat16)
        eye[...] = one_hot(256, 256, lambda r, q: r == q)

        def turn(i, _):
            r0 = pl.multiple_of((i // 4) * 256, 256)
            n0 = pl.multiple_of(lax.rem(i, 4) * 256, 256)
            inv[pl.ds(n0, 256), pl.ds(r0, 256)] = dot_t(
                eye[...], fwd[pl.ds(r0, 256), pl.ds(n0, 256)]
            ).astype(jnp.bfloat16)
            return 0

        lax.fori_loop(0, 16, turn, 0)
        ld_damp.wait()

    last = nchunk - 1
    ld_fwd.wait()
    ld_air[0].wait()
    dft(0)
    pl.semaphore_wait(barrier, NZ - 1 + NP - 1)
    z_start(0, 0, zs1[0], zr1[0])
    surface_flux()
    flip_copy(0, fpair).start()
    for j in range(1, nchunk):
        dft(j)
        if j < WINDOW:
            z_start(0, j, zs1[j], zr1[j])
    flip_copy(0, fpair).wait()
    spread_start(0, fpair, fall)
    prepare()
    find_routes()
    ocean_prepare()

    def step_a(j):
        z_wait(0, j, zs1[j], zr1[j])
        if j + WINDOW <= last:
            z_start(0, j + WINDOW, zs1[j + WINDOW], zr1[j + WINDOW])
        perm1(j)
        p_start(1, j, ps1[j], mid[j])

    def step_b(j):
        p_wait(1, j, ps1[j], mid[j])
        middle(j)
        p_start(2, j, ret[j], pr2[j])

    def step_c(j):
        p_wait(2, j, pr2[j], pr2[j])
        perm2(j)
        z_start(3, j, zs2[j], fin[j])

    def step_d(j):
        z_wait(3, j, zs2[j], fin[j])
        inverse(j)

    for i in range(nchunk + 3):
        if 0 <= i < nchunk:
            step_a(i)
        if i == 0:
            ocean_all()
        if i == 1:
            flip_copy(1, spair).wait()
            spread_start(1, spair, sall)
        if i == 3:
            place_sea()
        if 0 <= i - 1 < nchunk:
            step_b(i - 1)
        if 0 <= i - 2 < nchunk:
            step_c(i - 2)
        if 0 <= i - 3 < nchunk:
            step_d(i - 3)

    spread_sent(0, fall)
    spread_sent(1, sall)
    pltpu.make_async_copy(ocean, ocean_hbm, xs_sem.at[0, 5]).wait()
    for j in range(nchunk):
        z_sent(0, j, zs1[j], zr1[j])
        p_sent(1, j, ps1[j])
        p_sent(2, j, pr2[j])
        z_sent(3, j, zs2[j], fin[j])
        pltpu.make_async_copy(airv[j], out_hbm.at[:, :, pl.ds(offs[j], CHUNKS[j])], out_sem.at[j]).wait()


def spectral(air, fwd, pol, damp, patch, *rest):
    bf = jnp.bfloat16
    n = len(CHUNKS)
    scratch = [
        pltpu.VMEM((N, N), bf), pltpu.VMEM((N, N), bf),
        pltpu.VMEM((2, LAT, LAT), bf), pltpu.VMEM((2, LAT, LAT), bf), pltpu.VMEM((2, LAT, LAT), bf),
        pltpu.VMEM((LAT, 768), jnp.float32), pltpu.VMEM((256, 256), bf), pltpu.VMEM((256, 256), bf),
    ]
    scratch += [pltpu.VMEM((2, N, w), bf) for w in CHUNKS]
    scratch += [pltpu.VMEM((NZ, 2, 128, w), bf) for w in CHUNKS]
    scratch += [pltpu.VMEM((NZ, 2, 128, w), bf) for w in CHUNKS]
    scratch += [pltpu.VMEM((NP, 2, 2, 16, w), bf) for w in CHUNKS]
    scratch += [pltpu.VMEM((2, 2, NP, 16, w), bf) for w in CHUNKS]
    scratch += [pltpu.VMEM((2, 2, NP, 16, w), bf) for w in CHUNKS]
    scratch += [pltpu.VMEM((NP, 2, 2, 16, w), bf) for w in CHUNKS]
    scratch += [pltpu.VMEM((NZ, 2, 128, w), bf) for w in CHUNKS]
    scratch += [pltpu.VMEM((NZ, 2, 128, w), bf) for w in CHUNKS]
    scratch += [
        pltpu.VMEM((6, 1032, 128), bf), pltpu.VMEM((6, 4, 264, 128), jnp.float32),
        pltpu.VMEM((256, 256), bf), pltpu.VMEM((32, 256), bf),
        pltpu.VMEM((2, 4, 2, 8, 256), bf), pltpu.VMEM((16, 2, 4, 2, 8, 256), bf),
        pltpu.VMEM((2, 16, 256), bf), pltpu.VMEM((16, 2, 16, 256), bf),
        pltpu.VMEM((2, N, 128), jnp.float32), pltpu.VMEM((6, 2, 128, 256), bf),
        pltpu.VMEM((128, 1152), bf), pltpu.VMEM((128, 128), bf), pltpu.VMEM((128, 8), bf),
        pltpu.VMEM((256, 256), bf), pltpu.SMEM((16,), jnp.int32),
    ]
    dma = pltpu.SemaphoreType.DMA
    scratch += [dma((4 + n,)), dma((n,)), dma((4, n)), dma((4, n)), dma((4, n)), dma((2, 6))]
    anys = pl.BlockSpec(memory_space=pl.ANY)
    vm = pl.BlockSpec(memory_space=pltpu.VMEM)
    sm = pl.BlockSpec(memory_space=pltpu.SMEM)
    return pl.pallas_call(
        spectral_kernel,
        out_shape=(jax.ShapeDtypeStruct(air.shape, bf), jax.ShapeDtypeStruct((6, 2, 128, 256), bf)),
        in_specs=[anys] * 5 + [vm] * 8 + [sm] * 2,
        out_specs=(anys, anys),
        scratch_shapes=scratch,
        compiler_params=pltpu.CompilerParams(
            collective_id=0, has_side_effects=True, vmem_limit_bytes=60 << 20
        ),
        name="spectral",
    )(air, fwd, pol, damp, patch, *rest)


def shards(
    air_field_lattice,
    associated_polynomial_matrix,
    harmonic_damping_factor,
    boundary_exchange_projector,
    warmth_response_factor,
    water_patch_fields,
    kernel_coefficients,
    local_exchange_matrix,
    patch_average_matrix,
    water_kernel_offset,
    water_readout_matrix,
    patch_holder_index,
    water_point_indicator,
    water_point_totals,
):
    advanced, ocean = spectral(
        air_field_lattice,
        jnp.asarray(basis_table()),
        associated_polynomial_matrix,
        harmonic_damping_factor,
        water_patch_fields.transpose(0, 3, 2, 1).reshape(6, 1032, 128),
        warmth_response_factor,
        boundary_exchange_projector.T,
        kernel_coefficients.reshape(9 * 128, 128),
        local_exchange_matrix,
        patch_average_matrix,
        water_kernel_offset[None, :],
        water_readout_matrix,
        water_point_indicator,
        water_point_totals,
        patch_holder_index.T,
    )
    return (advanced, ocean.transpose(0, 2, 1, 3))


def solution(mesh):
    placed = (
        P(("sec", "band", "ch"), None, None),
        P(("sec", "band", "ch"), None, None),
        P(),
        P(),
        P(),
        P(("sec", "band", "ch"), None, None, None),
        P(),
        P(),
        P(),
        P(),
        P(),
        P(),
        P(("sec", "band", "ch"), None, None),
        P(("sec", "band", "ch")),
    )
    return jax.shard_map(
        shards,
        mesh=mesh,
        in_specs=placed,
        out_specs=(
            P(("sec", "band", "ch"), None, None),
            P(("sec", "band", "ch"), None, None, None),
        ),
        check_vma=False,
    )
```

```python
import functools
import math

import jax
import jax.numpy as jnp
import numpy as np
from jax import lax
from jax.experimental import pallas as pl
from jax.experimental.pallas import tpu as pltpu
from jax.sharding import PartitionSpec as P

MESH = pl.DeviceIdType.MESH
CHUNKS = (128,) * 6
WINDOW = 3
LAG = 4
OCEAN_AT = 1
NZ, NY, NX, NC = 8, 4, 4, 2
NP = NY * NX * NC
N = 1024
LAT = 512


def basis_table():
    z_hi, z_lo, part, y, low = np.meshgrid(
        np.arange(2), np.arange(4), np.arange(2), np.arange(4), np.arange(16), indexing="ij"
    )
    k = (z_lo * 128 + y * 32 + z_hi * 16 + low).reshape(-1)[:, None]
    angle = ((k * np.arange(N)[None, :]) % N).astype(np.float64) * (2.0 * math.pi / N)
    table = np.where(part.reshape(-1)[:, None] == 0, np.cos(angle), -np.sin(angle))
    return table.astype(np.float32).astype(jnp.bfloat16)


def one_hot(rows, cols, fn):
    r = lax.broadcasted_iota(jnp.int32, (rows, cols), 0)
    c = lax.broadcasted_iota(jnp.int32, (rows, cols), 1)
    return jnp.where(fn(r, c), 1.0, 0.0).astype(jnp.bfloat16)


def true_lat(i):
    t = i & 1
    z_lo = (i >> 1) & 3
    z_hi = (i >> 3) & 1
    c = (i >> 4) & 1
    x = (i >> 5) & 3
    y = (i >> 7) & 3
    return (z_lo * 64 + y * 16 + z_hi * 8 + x * 2 + c) * 2 + t


def spectral_kernel(
    air_hbm, fwd_hbm, pol_hbm, damp_hbm, patch_hbm, warm_ref, proj_ref, conv_ref,
    local_ref, mean_ref, bias_ref, read_ref, wet_ref, total_ref, owner_ref,
    out_hbm, ocean_hbm, *scr
):
    nchunk = len(CHUNKS)
    it = iter(scr)
    fwd, inv, pol, polp, polt, damp, q1, q2 = (next(it) for _ in range(8))
    airv = [next(it) for _ in CHUNKS]
    zs1 = [next(it) for _ in CHUNKS]
    zr1 = [next(it) for _ in CHUNKS]
    ps1 = [next(it) for _ in CHUNKS]
    mid = [next(it) for _ in CHUNKS]
    ret = [next(it) for _ in CHUNKS]
    pr2 = [next(it) for _ in CHUNKS]
    zs2 = [next(it) for _ in CHUNKS]
    fin = [next(it) for _ in CHUNKS]
    patch, x3, q3, q4, fpair, fall, spair, sall, seab, ocean = (next(it) for _ in range(10))
    conv_t, read_t, local_t, eye, q5, route = (next(it) for _ in range(6))
    load_sem, out_sem, send_sem, recv_sem, self_sem, xs_sem = (next(it) for _ in range(6))

    s = lax.axis_index("sec")
    b = lax.axis_index("band")
    c = lax.axis_index("ch")
    y = b // 8
    z_hi = lax.rem(b // 4, 2)
    x = lax.rem(b, 4)
    z = z_hi * 4 + s
    p = y * 8 + x * 2 + c
    yx = y * 4 + x

    def z_dev(zz):
        return (lax.rem(zz, 4), y * 8 + (zz // 4) * 4 + x, c)

    def p_dev(pp):
        return (s, (pp // 8) * 8 + z_hi * 4 + lax.rem(pp // 2, 4), lax.rem(pp, 2))

    offs = [0]
    for w in CHUNKS:
        offs.append(offs[-1] + w)

    loads = []

    def load(src, dst):
        copy = pltpu.make_async_copy(src, dst, load_sem.at[len(loads)])
        copy.start()
        loads.append(copy)
        return copy

    ld_fwd = load(fwd_hbm, fwd)
    ld_air = [load(air_hbm.at[:, :, pl.ds(offs[j], CHUNKS[j])], airv[j]) for j in range(nchunk)]
    ld_pol = load(pol_hbm, pol)
    ld_damp = load(damp_hbm, damp)
    ld_patch = load(patch_hbm, patch)

    barrier = pltpu.get_barrier_semaphore()

    def greet_z(i, _):
        pl.semaphore_signal(barrier, inc=1, device_id=z_dev(lax.rem(z + i, NZ)), device_id_type=MESH)
        return 0

    def greet_p(i, _):
        pl.semaphore_signal(barrier, inc=1, device_id=p_dev(lax.rem(p + i, NP)), device_id_type=MESH)
        return 0

    lax.fori_loop(1, NZ, greet_z, 0)
    lax.fori_loop(1, NP, greet_p, 0)

    def z_copy(stage, j, src, dst, i):
        near = (i + 1) // 2
        to = lax.rem(z + jnp.where(lax.rem(i, 2) == 1, near, NZ - near), NZ)
        return pltpu.make_async_remote_copy(
            src_ref=src.at[to], dst_ref=dst.at[z],
            send_sem=send_sem.at[stage, j], recv_sem=recv_sem.at[stage, j],
            device_id=z_dev(to), device_id_type=MESH,
        )

    def z_start(stage, j, src, dst):
        pltpu.make_async_copy(src.at[z], dst.at[z], self_sem.at[stage, j]).start()

        def go(i, _):
            z_copy(stage, j, src, dst, i).start()
            return 0

        lax.fori_loop(1, NZ, go, 0)

    def z_wait(stage, j, src, dst):
        pltpu.make_async_copy(src.at[z], dst.at[z], self_sem.at[stage, j]).wait()
        pltpu.make_async_copy(src.at[pl.ds(0, NZ - 1)], dst.at[pl.ds(0, NZ - 1)], recv_sem.at[stage, j]).wait()

    def z_sent(stage, j, src, dst):
        pltpu.make_async_copy(src.at[pl.ds(0, NZ - 1)], dst.at[pl.ds(0, NZ - 1)], send_sem.at[stage, j]).wait()

    def p_start(stage, j, src, dst):
        def pick(to):
            if stage == 1:
                return src.at[to], dst.at[:, :, p]
            return src.at[:, :, to], dst.at[p]

        a, d = pick(p)
        pltpu.make_async_copy(a, d, self_sem.at[stage, j]).start()

        def go(i, _):
            to = lax.rem(p + i, NP)
            a, d = pick(to)
            pltpu.make_async_remote_copy(
                src_ref=a, dst_ref=d, send_sem=send_sem.at[stage, j], recv_sem=recv_sem.at[stage, j],
                device_id=p_dev(to), device_id_type=MESH,
            ).start()
            return 0

        lax.fori_loop(1, NP, go, 0)

    def p_wait(stage, j, flat, whole):
        a = flat.at[0]
        pltpu.make_async_copy(a, a, self_sem.at[stage, j]).wait()
        a = flat.at[pl.ds(0, NP - 1)]
        pltpu.make_async_copy(a, a, recv_sem.at[stage, j]).wait()

    def p_sent(stage, j, flat):
        a = flat.at[pl.ds(0, NP - 1)]
        pltpu.make_async_copy(a, a, send_sem.at[stage, j]).wait()

    def dot(a, bb):
        return jnp.dot(a, bb, preferred_element_type=jnp.float32)

    def flip_copy(stage, buf):
        return pltpu.make_async_remote_copy(
            src_ref=buf.at[z_hi], dst_ref=buf.at[z_hi], send_sem=xs_sem.at[stage, 0], recv_sem=xs_sem.at[stage, 1],
            device_id=z_dev(lax.rem(z + 4, NZ)), device_id_type=MESH,
        )

    def spread_start(stage, pair, whole):
        pltpu.make_async_copy(pair, whole.at[yx], xs_sem.at[stage, 2]).start()

        def go(i, _):
            to = lax.rem(yx + i, 16)
            pltpu.make_async_remote_copy(
                src_ref=pair, dst_ref=whole.at[yx], send_sem=xs_sem.at[stage, 3], recv_sem=xs_sem.at[stage, 4],
                device_id=p_dev(to * 2 + c), device_id_type=MESH,
            ).start()
            return 0

        lax.fori_loop(1, 16, go, 0)

    def spread_wait(stage, pair, whole):
        pltpu.make_async_copy(pair, whole.at[yx], xs_sem.at[stage, 2]).wait()
        a = whole.at[pl.ds(0, 15)]
        pltpu.make_async_copy(a, a, xs_sem.at[stage, 4]).wait()

    def spread_sent(stage, whole):
        a = whole.at[pl.ds(0, 15)]
        pltpu.make_async_copy(a, a, xs_sem.at[stage, 3]).wait()

    def dot_t(a, bb):
        return lax.dot_general(a, bb, (((1,), (1,)), ((), ())), preferred_element_type=jnp.float32)

    def surface_flux():
        for j in range(nchunk):
            ld_air[j].wait() if j else None
        for t in range(2):
            acc = None
            for j in range(nchunk):
                part = dot_t(proj_ref[:, offs[j]:offs[j] + CHUNKS[j]], airv[j][t])
                acc = part if acc is None else acc + part
            acc = acc.astype(jnp.bfloat16)
            for q in range(4):
                fpair[z_hi, q, t] = acc[:, q * 256:(q + 1) * 256]

    def rows_first(i, _):
        for blk in range(4):
            rows = patch[i, blk * 256:(blk + 1) * 256, :]
            x3[i, :, blk * 64:(blk + 1) * 64, :] = dot(q3[...], rows).reshape(4, 64, 128)
        x3[i, :, 256:264, :] = dot(q4[...], patch[i, 776:1032, :]).reshape(4, 8, 128)
        return 0

    def ocean_step(i, sea):
        tile = route[i]
        owner_b = tile >> 2
        flux = fall[((owner_b >> 3) << 2) + (owner_b & 3), (owner_b >> 2) & 1, tile & 3].astype(jnp.float32)
        wet = wet_ref[i].astype(jnp.float32)
        masked = [flux[r] * wet[r:r + 1, :] for r in range(2)]
        whole = jnp.sum(masked[0] + masked[1], axis=1, keepdims=True)
        fmean = whole / jnp.maximum(total_ref[i].astype(jnp.float32), 1.0)
        row = jnp.sum(mean_ref[...] * fmean, axis=0, keepdims=True) + bias_ref[...]
        shift = jnp.broadcast_to(row, (128, 128)).T
        shift = jnp.concatenate([shift, shift], axis=1)
        fresh = []
        for r in range(2):
            wins = [
                x3[i, r + dr, dw:dw + 256, :].astype(jnp.bfloat16) for dr in range(3) for dw in range(3)
            ]
            pre = dot_t(conv_t[...], jnp.concatenate(wins, axis=1))
            pre = pre + dot(local_t[...], masked[r].astype(jnp.bfloat16)) + shift
            hidden = jax.nn.gelu(pre, approximate=True).astype(jnp.bfloat16)
            old = dot_t(eye[:128, :128], wins[4])
            new = (old + dot(read_t[...], hidden)) * wet[r:r + 1, :]
            fresh.append(new.astype(jnp.bfloat16))
            line = lax.broadcasted_iota(jnp.int32, (16, 256), 0)
            sea = jnp.where(line == 2 * i + r, jnp.broadcast_to(new[0:1, :], (16, 256)), sea)
        quarters = [fresh[r][:, h * 128:(h + 1) * 128] for h in range(2) for r in range(2)]
        ocean[i] = dot(q5[...], jnp.concatenate(quarters, axis=0)).astype(jnp.bfloat16)
        return sea

    def ocean_prepare():
        q3[...] = one_hot(256, 256, lambda r, q: ((r >> 6) == (q & 3)) & ((r & 63) == (q >> 2)))
        q4[...] = one_hot(32, 256, lambda r, q: q == (r & 7) * 4 + (r >> 3) + 248)
        q5[...] = one_hot(512, 512, lambda r, q: ((r >> 2) == (q & 127)) & ((r & 3) == (q >> 7)))
        small = eye[:128, :128]
        conv_t[...] = dot_t(small, conv_ref[...]).astype(jnp.bfloat16)
        read_t[...] = dot_t(small, read_ref[...]).astype(jnp.bfloat16)
        local_t[...] = dot_t(small, local_ref[...]).astype(jnp.bfloat16)
        ld_patch.wait()
        lax.fori_loop(0, 6, rows_first, 0)

    def find_routes():
        mine = [owner_ref[q, (s * 32 + b) * 2 + c] for q in range(4)]

        def scan(i, held):
            held = list(held)
            for q in range(4):
                owner = owner_ref[q, (s * 32 + i) * 2 + c]
                hit = owner == b
                for k in range(6):
                    held[k] = jnp.where(hit & (held[6] == k), i * 4 + q, held[k])
                held[6] = held[6] + jnp.where(hit, 1, 0)
                for k in range(4):
                    before = i * 4 + q < b * 4 + k
                    held[7 + k] = held[7 + k] + jnp.where((owner == mine[k]) & before, 1, 0)
            return tuple(held)

        held = lax.fori_loop(0, 32, scan, tuple(jnp.int32(0) for _ in range(11)))
        for k in range(6):
            route[k] = held[k]
        for k in range(4):
            route[8 + k] = mine[k]
            route[12 + k] = held[7 + k]

    def ocean_all():
        spread_wait(0, fpair, fall)
        sea = lax.fori_loop(0, 6, ocean_step, jnp.zeros((16, 256), jnp.float32))
        spair[z_hi] = sea.astype(jnp.bfloat16)
        flip_copy(1, spair).start()
        pltpu.make_async_copy(ocean, ocean_hbm, xs_sem.at[0, 5]).start()

    def place_sea():
        spread_wait(1, spair, sall)
        for q in range(4):
            owner = route[8 + q]
            slot = route[12 + q]
            tile = sall[((owner >> 3) << 2) + (owner & 3), (owner >> 2) & 1].astype(jnp.float32)
            for t in range(2):
                line = lax.broadcasted_iota(jnp.int32, (16, 256), 0)
                row = jnp.sum(jnp.where(line == 2 * slot + t, tile, 0.0), axis=0, keepdims=True)
                seab[t, q * 256:(q + 1) * 256, :] = jnp.broadcast_to(row, (128, 256)).T

    def pair(a, bb):
        return jnp.concatenate([a, bb], axis=1)

    def dft(j):
        w = CHUNKS[j]

        def body(m, _):
            rows = fwd[pl.ds(pl.multiple_of(m * 256, 256), 256), :]
            f = dot(rows, pair(airv[j][0], airv[j][1])).astype(jnp.bfloat16)
            for t in range(2):
                zs1[j][pl.ds(m * 2, 2), t] = f[:, t * w:(t + 1) * w].reshape(2, 128, w)
            return 0

        lax.fori_loop(0, 4, body, 0)

    def perm1(j):
        w = CHUNKS[j]

        def body(g, _):
            r0 = pl.multiple_of(g * 16, 16)
            xin = pair(
                zr1[j][:, :, pl.ds(r0, 16), :].reshape(256, w),
                zr1[j][:, :, pl.ds(r0 + 64, 16), :].reshape(256, w),
            )
            yo = dot(q1[...], xin).astype(jnp.bfloat16)
            for part in range(2):
                ps1[j][pl.ds(g * 8, 8), part] = yo[:, part * w:(part + 1) * w].reshape(8, 2, 16, w)
            return 0

        lax.fori_loop(0, 4, body, 0)

    def middle(j):
        w = CHUNKS[j]
        d0 = offs[j]

        def body(k, _):
            xin = pair(mid[j][0, k].reshape(LAT, w), mid[j][1, k].reshape(LAT, w))
            sp = dot(polp[k], xin)
            dm = damp[:, d0:d0 + w]
            sc = (sp * pair(dm, dm)).astype(jnp.bfloat16)
            fo = dot(polt[k], sc).astype(jnp.bfloat16)
            for part in range(2):
                ret[j][part, k] = fo[:, part * w:(part + 1) * w].reshape(NP, 16, w)
            return 0

        lax.fori_loop(0, 2, body, 0)

    def perm2(j):
        w = CHUNKS[j]

        def body(g, _):
            r0 = pl.multiple_of(g * 16, 16)
            xin = pair(
                pr2[j][pl.ds(g * 8, 8), 0].reshape(256, w),
                pr2[j][pl.ds(g * 8, 8), 1].reshape(256, w),
            )
            yo = dot(q2[...], xin).astype(jnp.bfloat16)
            for part in range(2):
                zs2[j][:, :, pl.ds(r0 + part * 64, 16), :] = yo[:, part * w:(part + 1) * w].reshape(8, 2, 16, w)
            return 0

        lax.fori_loop(0, 4, body, 0)

    def inverse(j):
        w = CHUNKS[j]
        d0 = offs[j]

        def body(i, _):
            m = pl.multiple_of(i * 256, 256)
            rows = inv[pl.ds(m, 256), :]
            rec = dot(rows, pair(fin[j][:, 0].reshape(N, w), fin[j][:, 1].reshape(N, w))) * (1.0 / 512.0)
            for t in range(2):
                old = airv[j][t, pl.ds(m, 256), :].astype(jnp.float32)
                sea = seab[t, pl.ds(m, 256), :]
                sea = jnp.concatenate([sea] * (w // 128), axis=1)
                new = old + rec[:, t * w:(t + 1) * w] + sea * warm_ref[d0:d0 + w][None, :]
                airv[j][t, pl.ds(m, 256), :] = new.astype(jnp.bfloat16)
            return 0

        lax.fori_loop(0, 4, body, 0)
        pltpu.make_async_copy(airv[j], out_hbm.at[:, :, pl.ds(d0, w)], out_sem.at[j]).start()

    def prepare():
        q1[...] = one_hot(256, 256, lambda r, q: (((r & 15) == (q >> 4)) & ((r >> 5) == ((q >> 1) & 7)) & (((r >> 4) & 1) == (q & 1))))
        q2[...] = one_hot(256, 256, lambda q, r: (((r & 15) == (q >> 4)) & ((r >> 5) == ((q >> 1) & 7)) & (((r >> 4) & 1) == (q & 1))))
        ld_pol.wait()
        sel = one_hot(LAT, LAT, lambda r, q: r == true_lat(q))
        selt = one_hot(LAT, LAT, lambda r, q: true_lat(r) == q)
        for k in range(2):
            polp[k] = dot(pol[k], sel).astype(jnp.bfloat16)
            polt[k] = lax.dot_general(
                selt, pol[k], (((1,), (1,)), ((), ())), preferred_element_type=jnp.float32
            ).astype(jnp.bfloat16)
        eye[...] = one_hot(256, 256, lambda r, q: r == q)

        def turn(i, _):
            r0 = pl.multiple_of((i // 4) * 256, 256)
            n0 = pl.multiple_of(lax.rem(i, 4) * 256, 256)
            inv[pl.ds(n0, 256), pl.ds(r0, 256)] = dot_t(
                eye[...], fwd[pl.ds(r0, 256), pl.ds(n0, 256)]
            ).astype(jnp.bfloat16)
            return 0

        lax.fori_loop(0, 16, turn, 0)
        ld_damp.wait()

    last = nchunk - 1
    ld_fwd.wait()
    ld_air[0].wait()
    dft(0)
    pl.semaphore_wait(barrier, NZ - 1 + NP - 1)
    z_start(0, 0, zs1[0], zr1[0])
    surface_flux()
    flip_copy(0, fpair).start()
    for j in range(1, nchunk):
        dft(j)
        if j < WINDOW:
            z_start(0, j, zs1[j], zr1[j])
    flip_copy(0, fpair).wait()
    spread_start(0, fpair, fall)
    prepare()
    find_routes()
    ocean_prepare()

    def step_a(j):
        z_wait(0, j, zs1[j], zr1[j])
        if j + WINDOW <= last:
            z_start(0, j + WINDOW, zs1[j + WINDOW], zr1[j + WINDOW])
        perm1(j)
        p_start(1, j, ps1[j], mid[j])

    def step_b(j):
        p_wait(1, j, ps1[j], mid[j])
        middle(j)
        p_start(2, j, ret[j], pr2[j])

    def step_c(j):
        p_wait(2, j, pr2[j], pr2[j])
        perm2(j)
        z_start(3, j, zs2[j], fin[j])

    def step_d(j):
        z_wait(3, j, zs2[j], fin[j])
        inverse(j)

    for i in range(nchunk + LAG):
        if i < nchunk:
            step_a(i)
        if i == OCEAN_AT:
            ocean_all()
        if i == OCEAN_AT + 1:
            flip_copy(1, spair).wait()
            spread_start(1, spair, sall)
        if 0 <= i - 1 < nchunk:
            step_b(i - 1)
        if 0 <= i - 2 < nchunk:
            step_c(i - 2)
        if i == LAG:
            place_sea()
        if 0 <= i - LAG < nchunk:
            step_d(i - LAG)

    spread_sent(0, fall)
    spread_sent(1, sall)
    pltpu.make_async_copy(ocean, ocean_hbm, xs_sem.at[0, 5]).wait()
    for j in range(nchunk):
        z_sent(0, j, zs1[j], zr1[j])
        p_sent(1, j, ps1[j])
        p_sent(2, j, pr2[j])
        z_sent(3, j, zs2[j], fin[j])
        pltpu.make_async_copy(airv[j], out_hbm.at[:, :, pl.ds(offs[j], CHUNKS[j])], out_sem.at[j]).wait()


def spectral(air, fwd, pol, damp, patch, *rest):
    bf = jnp.bfloat16
    n = len(CHUNKS)
    scratch = [
        pltpu.VMEM((N, N), bf), pltpu.VMEM((N, N), bf),
        pltpu.VMEM((2, LAT, LAT), bf), pltpu.VMEM((2, LAT, LAT), bf), pltpu.VMEM((2, LAT, LAT), bf),
        pltpu.VMEM((LAT, 768), jnp.float32), pltpu.VMEM((256, 256), bf), pltpu.VMEM((256, 256), bf),
    ]
    scratch += [pltpu.VMEM((2, N, w), bf) for w in CHUNKS]
    scratch += [pltpu.VMEM((NZ, 2, 128, w), bf) for w in CHUNKS]
    scratch += [pltpu.VMEM((NZ, 2, 128, w), bf) for w in CHUNKS]
    scratch += [pltpu.VMEM((NP, 2, 2, 16, w), bf) for w in CHUNKS]
    scratch += [pltpu.VMEM((2, 2, NP, 16, w), bf) for w in CHUNKS]
    scratch += [pltpu.VMEM((2, 2, NP, 16, w), bf) for w in CHUNKS]
    scratch += [pltpu.VMEM((NP, 2, 2, 16, w), bf) for w in CHUNKS]
    scratch += [pltpu.VMEM((NZ, 2, 128, w), bf) for w in CHUNKS]
    scratch += [pltpu.VMEM((NZ, 2, 128, w), bf) for w in CHUNKS]
    scratch += [
        pltpu.VMEM((6, 1032, 128), bf), pltpu.VMEM((6, 4, 264, 128), jnp.float32),
        pltpu.VMEM((256, 256), bf), pltpu.VMEM((32, 256), bf),
        pltpu.VMEM((2, 4, 2, 8, 256), bf), pltpu.VMEM((16, 2, 4, 2, 8, 256), bf),
        pltpu.VMEM((2, 16, 256), bf), pltpu.VMEM((16, 2, 16, 256), bf),
        pltpu.VMEM((2, N, 128), jnp.float32), pltpu.VMEM((6, 512, 128), bf),
        pltpu.VMEM((128, 1152), bf), pltpu.VMEM((128, 128), bf), pltpu.VMEM((128, 8), bf),
        pltpu.VMEM((256, 256), bf), pltpu.VMEM((512, 512), bf), pltpu.SMEM((16,), jnp.int32),
    ]
    dma = pltpu.SemaphoreType.DMA
    scratch += [dma((4 + n,)), dma((n,)), dma((4, n)), dma((4, n)), dma((4, n)), dma((2, 6))]
    anys = pl.BlockSpec(memory_space=pl.ANY)
    vm = pl.BlockSpec(memory_space=pltpu.VMEM)
    sm = pl.BlockSpec(memory_space=pltpu.SMEM)
    return pl.pallas_call(
        spectral_kernel,
        out_shape=(jax.ShapeDtypeStruct(air.shape, bf), jax.ShapeDtypeStruct((6, 512, 128), bf)),
        in_specs=[anys] * 5 + [vm] * 8 + [sm] * 2,
        out_specs=(anys, anys),
        scratch_shapes=scratch,
        compiler_params=pltpu.CompilerParams(
            collective_id=0, has_side_effects=True, vmem_limit_bytes=60 << 20
        ),
        name="spectral",
    )(air, fwd, pol, damp, patch, *rest)


def shards(
    air_field_lattice,
    associated_polynomial_matrix,
    harmonic_damping_factor,
    boundary_exchange_projector,
    warmth_response_factor,
    water_patch_fields,
    kernel_coefficients,
    local_exchange_matrix,
    patch_average_matrix,
    water_kernel_offset,
    water_readout_matrix,
    patch_holder_index,
    water_point_indicator,
    water_point_totals,
):
    advanced, ocean = spectral(
        air_field_lattice,
        jnp.asarray(basis_table()),
        associated_polynomial_matrix,
        harmonic_damping_factor,
        water_patch_fields.transpose(0, 3, 2, 1).reshape(6, 1032, 128),
        warmth_response_factor,
        boundary_exchange_projector.T,
        kernel_coefficients.reshape(9 * 128, 128),
        local_exchange_matrix,
        patch_average_matrix,
        water_kernel_offset[None, :],
        water_readout_matrix,
        water_point_indicator,
        water_point_totals,
        patch_holder_index.T,
    )
    ocean = ocean.reshape(6, 128, 2, 2, 128).transpose(0, 1, 3, 2, 4).reshape(6, 128, 2, 256)
    return (advanced, ocean)


def solution(mesh):
    placed = (
        P(("sec", "band", "ch"), None, None),
        P(("sec", "band", "ch"), None, None),
        P(),
        P(),
        P(),
        P(("sec", "band", "ch"), None, None, None),
        P(),
        P(),
        P(),
        P(),
        P(),
        P(),
        P(("sec", "band", "ch"), None, None),
        P(("sec", "band", "ch")),
    )
    return jax.shard_map(
        shards,
        mesh=mesh,
        in_specs=placed,
        out_specs=(
            P(("sec", "band", "ch"), None, None),
            P(("sec", "band", "ch"), None, None, None),
        ),
        check_vma=False,
    )
```

```python
import functools
import math

import jax
import jax.numpy as jnp
import numpy as np
from jax import lax
from jax.experimental import pallas as pl
from jax.experimental.pallas import tpu as pltpu
from jax.sharding import PartitionSpec as P

MESH = pl.DeviceIdType.MESH
CHUNKS = (128,) * 6
WINDOW = 3
LAG = 4
OCEAN_AT = 1
START = 3
PIECES = 8
HAND = 1
NZ, NY, NX, NC = 8, 4, 4, 2
NP = NY * NX * NC
N = 1024
LAT = 512


def basis_table():
    z_hi, z_lo, part, y, low = np.meshgrid(
        np.arange(2), np.arange(4), np.arange(2), np.arange(4), np.arange(16), indexing="ij"
    )
    k = (z_lo * 128 + y * 32 + z_hi * 16 + low).reshape(-1)[:, None]
    angle = ((k * np.arange(N)[None, :]) % N).astype(np.float64) * (2.0 * math.pi / N)
    table = np.where(part.reshape(-1)[:, None] == 0, np.cos(angle), -np.sin(angle))
    return table.astype(np.float32).astype(jnp.bfloat16)


def one_hot(rows, cols, fn):
    r = lax.broadcasted_iota(jnp.int32, (rows, cols), 0)
    c = lax.broadcasted_iota(jnp.int32, (rows, cols), 1)
    return jnp.where(fn(r, c), 1.0, 0.0).astype(jnp.bfloat16)


def true_lat(i):
    t = i & 1
    z_lo = (i >> 1) & 3
    z_hi = (i >> 3) & 1
    c = (i >> 4) & 1
    x = (i >> 5) & 3
    y = (i >> 7) & 3
    return (z_lo * 64 + y * 16 + z_hi * 8 + x * 2 + c) * 2 + t


def spectral_kernel(
    air_hbm, fwd_hbm, pol_hbm, damp_hbm, patch_hbm, warm_ref, proj_ref, conv_ref,
    local_ref, mean_ref, bias_ref, read_ref, wet_ref, total_ref, owner_ref,
    out_hbm, ocean_hbm, *scr
):
    nchunk = len(CHUNKS)
    it = iter(scr)
    fwd, inv, pol, polp, polt, damp, q1, q2 = (next(it) for _ in range(8))
    airv = [next(it) for _ in CHUNKS]
    zs1 = [next(it) for _ in CHUNKS]
    zr1 = [next(it) for _ in CHUNKS]
    ps1 = [next(it) for _ in CHUNKS]
    mid = [next(it) for _ in CHUNKS]
    ret = [next(it) for _ in CHUNKS]
    pr2 = [next(it) for _ in CHUNKS]
    zs2 = [next(it) for _ in CHUNKS]
    fin = [next(it) for _ in CHUNKS]
    patch, x3, q3, q4, fpair, fall, spair, sall, seab, ocean = (next(it) for _ in range(10))
    conv_t, read_t, local_t, eye, q5, route = (next(it) for _ in range(6))
    load_sem, out_sem, send_sem, recv_sem, self_sem, xs_sem = (next(it) for _ in range(6))

    s = lax.axis_index("sec")
    b = lax.axis_index("band")
    c = lax.axis_index("ch")
    y = b // 8
    z_hi = lax.rem(b // 4, 2)
    x = lax.rem(b, 4)
    z = z_hi * 4 + s
    p = y * 8 + x * 2 + c
    yx = y * 4 + x

    def z_dev(zz):
        return (lax.rem(zz, 4), y * 8 + (zz // 4) * 4 + x, c)

    def p_dev(pp):
        return (s, (pp // 8) * 8 + z_hi * 4 + lax.rem(pp // 2, 4), lax.rem(pp, 2))

    offs = [0]
    for w in CHUNKS:
        offs.append(offs[-1] + w)

    loads = []

    def load(src, dst):
        copy = pltpu.make_async_copy(src, dst, load_sem.at[len(loads)])
        copy.start()
        loads.append(copy)
        return copy

    ld_fwd = load(fwd_hbm, fwd)
    ld_air = [load(air_hbm.at[:, :, pl.ds(offs[j], CHUNKS[j])], airv[j]) for j in range(nchunk)]
    ld_pol = load(pol_hbm, pol)
    ld_damp = load(damp_hbm, damp)
    ld_patch = load(patch_hbm, patch)

    barrier = pltpu.get_barrier_semaphore()

    def greet_z(i, _):
        pl.semaphore_signal(barrier, inc=1, device_id=z_dev(lax.rem(z + i, NZ)), device_id_type=MESH)
        return 0

    def greet_p(i, _):
        pl.semaphore_signal(barrier, inc=1, device_id=p_dev(lax.rem(p + i, NP)), device_id_type=MESH)
        return 0

    lax.fori_loop(1, NZ, greet_z, 0)
    lax.fori_loop(1, NP, greet_p, 0)

    def z_copy(stage, j, src, dst, i):
        near = (i + 1) // 2
        to = lax.rem(z + jnp.where(lax.rem(i, 2) == 1, near, NZ - near), NZ)
        return pltpu.make_async_remote_copy(
            src_ref=src.at[to], dst_ref=dst.at[z],
            send_sem=send_sem.at[stage, j], recv_sem=recv_sem.at[stage, j],
            device_id=z_dev(to), device_id_type=MESH,
        )

    def z_start(stage, j, src, dst):
        pltpu.make_async_copy(src.at[z], dst.at[z], self_sem.at[stage, j]).start()

        def go(i, _):
            z_copy(stage, j, src, dst, i).start()
            return 0

        lax.fori_loop(1, NZ, go, 0)

    def z_wait(stage, j, src, dst):
        pltpu.make_async_copy(src.at[z], dst.at[z], self_sem.at[stage, j]).wait()
        pltpu.make_async_copy(src.at[pl.ds(0, NZ - 1)], dst.at[pl.ds(0, NZ - 1)], recv_sem.at[stage, j]).wait()

    def z_sent(stage, j, src, dst):
        pltpu.make_async_copy(src.at[pl.ds(0, NZ - 1)], dst.at[pl.ds(0, NZ - 1)], send_sem.at[stage, j]).wait()

    def p_start(stage, j, src, dst):
        def pick(to):
            if stage == 1:
                return src.at[to], dst.at[:, :, p]
            return src.at[:, :, to], dst.at[p]

        a, d = pick(p)
        pltpu.make_async_copy(a, d, self_sem.at[stage, j]).start()

        def go(i, _):
            to = lax.rem(p + i, NP)
            a, d = pick(to)
            pltpu.make_async_remote_copy(
                src_ref=a, dst_ref=d, send_sem=send_sem.at[stage, j], recv_sem=recv_sem.at[stage, j],
                device_id=p_dev(to), device_id_type=MESH,
            ).start()
            return 0

        lax.fori_loop(1, NP, go, 0)

    def p_wait(stage, j, flat, whole):
        a = flat.at[0]
        pltpu.make_async_copy(a, a, self_sem.at[stage, j]).wait()
        a = flat.at[pl.ds(0, NP - 1)]
        pltpu.make_async_copy(a, a, recv_sem.at[stage, j]).wait()

    def p_sent(stage, j, flat):
        a = flat.at[pl.ds(0, NP - 1)]
        pltpu.make_async_copy(a, a, send_sem.at[stage, j]).wait()

    def dot(a, bb):
        return jnp.dot(a, bb, preferred_element_type=jnp.float32)

    def flip_copy(stage, buf):
        return pltpu.make_async_remote_copy(
            src_ref=buf.at[z_hi], dst_ref=buf.at[z_hi], send_sem=xs_sem.at[stage, 0], recv_sem=xs_sem.at[stage, 1],
            device_id=z_dev(lax.rem(z + 4, NZ)), device_id_type=MESH,
        )

    def spread_start(stage, pair, whole):
        pltpu.make_async_copy(pair, whole.at[yx], xs_sem.at[stage, 2]).start()

        def go(i, _):
            to = lax.rem(yx + i, 16)
            pltpu.make_async_remote_copy(
                src_ref=pair, dst_ref=whole.at[yx], send_sem=xs_sem.at[stage, 3], recv_sem=xs_sem.at[stage, 4],
                device_id=p_dev(to * 2 + c), device_id_type=MESH,
            ).start()
            return 0

        lax.fori_loop(1, 16, go, 0)

    def spread_wait(stage, pair, whole):
        pltpu.make_async_copy(pair, whole.at[yx], xs_sem.at[stage, 2]).wait()
        a = whole.at[pl.ds(0, 15)]
        pltpu.make_async_copy(a, a, xs_sem.at[stage, 4]).wait()

    def spread_sent(stage, whole):
        a = whole.at[pl.ds(0, 15)]
        pltpu.make_async_copy(a, a, xs_sem.at[stage, 3]).wait()

    def dot_t(a, bb):
        return lax.dot_general(a, bb, (((1,), (1,)), ((), ())), preferred_element_type=jnp.float32)

    def surface_flux():
        for j in range(nchunk):
            ld_air[j].wait() if j else None
        for t in range(2):
            acc = None
            for j in range(nchunk):
                part = dot_t(proj_ref[:, offs[j]:offs[j] + CHUNKS[j]], airv[j][t])
                acc = part if acc is None else acc + part
            acc = acc.astype(jnp.bfloat16)
            for q in range(4):
                fpair[z_hi, q, t] = acc[:, q * 256:(q + 1) * 256]

    def rows_first(i, _):
        for blk in range(4):
            rows = patch[i, blk * 256:(blk + 1) * 256, :]
            x3[i, :, blk * 64:(blk + 1) * 64, :] = dot(q3[...], rows).reshape(4, 64, 128)
        x3[i, :, 256:264, :] = dot(q4[...], patch[i, 776:1032, :]).reshape(4, 8, 128)
        return 0

    def ocean_step(i, sea):
        tile = route[i]
        owner_b = tile >> 2
        flux = fall[((owner_b >> 3) << 2) + (owner_b & 3), (owner_b >> 2) & 1, tile & 3].astype(jnp.float32)
        wet = wet_ref[i].astype(jnp.float32)
        masked = [flux[r] * wet[r:r + 1, :] for r in range(2)]
        whole = jnp.sum(masked[0] + masked[1], axis=1, keepdims=True)
        fmean = whole / jnp.maximum(total_ref[i].astype(jnp.float32), 1.0)
        row = jnp.sum(mean_ref[...] * fmean, axis=0, keepdims=True) + bias_ref[...]
        shift = jnp.broadcast_to(row, (128, 128)).T
        shift = jnp.concatenate([shift, shift], axis=1)
        fresh = []
        for r in range(2):
            wins = [
                x3[i, r + dr, dw:dw + 256, :].astype(jnp.bfloat16) for dr in range(3) for dw in range(3)
            ]
            pre = dot_t(conv_t[...], jnp.concatenate(wins, axis=1))
            pre = pre + dot(local_t[...], masked[r].astype(jnp.bfloat16)) + shift
            hidden = jax.nn.gelu(pre, approximate=True).astype(jnp.bfloat16)
            old = dot_t(eye[:128, :128], wins[4])
            new = (old + dot(read_t[...], hidden)) * wet[r:r + 1, :]
            fresh.append(new.astype(jnp.bfloat16))
            line = lax.broadcasted_iota(jnp.int32, (16, 256), 0)
            sea = jnp.where(line == 2 * i + r, jnp.broadcast_to(new[0:1, :], (16, 256)), sea)
        quarters = [fresh[r][:, h * 128:(h + 1) * 128] for h in range(2) for r in range(2)]
        ocean[i] = dot(q5[...], jnp.concatenate(quarters, axis=0)).astype(jnp.bfloat16)
        return sea

    def ocean_prepare():
        q3[...] = one_hot(256, 256, lambda r, q: ((r >> 6) == (q & 3)) & ((r & 63) == (q >> 2)))
        q4[...] = one_hot(32, 256, lambda r, q: q == (r & 7) * 4 + (r >> 3) + 248)
        q5[...] = one_hot(512, 512, lambda r, q: ((r >> 2) == (q & 127)) & ((r & 3) == (q >> 7)))
        small = eye[:128, :128]
        conv_t[...] = dot_t(small, conv_ref[...]).astype(jnp.bfloat16)
        read_t[...] = dot_t(small, read_ref[...]).astype(jnp.bfloat16)
        local_t[...] = dot_t(small, local_ref[...]).astype(jnp.bfloat16)
        ld_patch.wait()
        lax.fori_loop(0, 6, rows_first, 0)

    def find_routes():
        mine = [owner_ref[q, (s * 32 + b) * 2 + c] for q in range(4)]

        def scan(i, held):
            held = list(held)
            for q in range(4):
                owner = owner_ref[q, (s * 32 + i) * 2 + c]
                hit = owner == b
                for k in range(6):
                    held[k] = jnp.where(hit & (held[6] == k), i * 4 + q, held[k])
                held[6] = held[6] + jnp.where(hit, 1, 0)
                for k in range(4):
                    before = i * 4 + q < b * 4 + k
                    held[7 + k] = held[7 + k] + jnp.where((owner == mine[k]) & before, 1, 0)
            return tuple(held)

        held = lax.fori_loop(0, 32, scan, tuple(jnp.int32(0) for _ in range(11)))
        for k in range(6):
            route[k] = held[k]
        for k in range(4):
            route[8 + k] = mine[k]
            route[12 + k] = held[7 + k]

    def ocean_all():
        spread_wait(0, fpair, fall)
        sea = lax.fori_loop(0, 6, ocean_step, jnp.zeros((16, 256), jnp.float32))
        spair[z_hi] = sea.astype(jnp.bfloat16)
        flip_copy(1, spair).start()
        pltpu.make_async_copy(ocean, ocean_hbm, xs_sem.at[0, 5]).start()

    def place_sea():
        spread_wait(1, spair, sall)
        for q in range(4):
            owner = route[8 + q]
            slot = route[12 + q]
            tile = sall[((owner >> 3) << 2) + (owner & 3), (owner >> 2) & 1].astype(jnp.float32)
            for t in range(2):
                line = lax.broadcasted_iota(jnp.int32, (16, 256), 0)
                row = jnp.sum(jnp.where(line == 2 * slot + t, tile, 0.0), axis=0, keepdims=True)
                seab[t, q * 256:(q + 1) * 256, :] = jnp.broadcast_to(row, (128, 256)).T

    def pair(a, bb):
        return jnp.concatenate([a, bb], axis=1)

    def dft(j):
        w = CHUNKS[j]

        def body(m, _):
            rows = fwd[pl.ds(pl.multiple_of(m * 256, 256), 256), :]
            f = dot(rows, pair(airv[j][0], airv[j][1])).astype(jnp.bfloat16)
            for t in range(2):
                zs1[j][pl.ds(m * 2, 2), t] = f[:, t * w:(t + 1) * w].reshape(2, 128, w)
            return 0

        lax.fori_loop(0, 4, body, 0)

    def perm1(j):
        w = CHUNKS[j]

        def body(g, _):
            r0 = pl.multiple_of(g * 16, 16)
            xin = pair(
                zr1[j][:, :, pl.ds(r0, 16), :].reshape(256, w),
                zr1[j][:, :, pl.ds(r0 + 64, 16), :].reshape(256, w),
            )
            yo = dot(q1[...], xin).astype(jnp.bfloat16)
            for part in range(2):
                ps1[j][pl.ds(g * 8, 8), part] = yo[:, part * w:(part + 1) * w].reshape(8, 2, 16, w)
            return 0

        lax.fori_loop(0, 4, body, 0)

    def middle(j):
        w = CHUNKS[j]
        d0 = offs[j]

        def body(k, _):
            xin = pair(mid[j][0, k].reshape(LAT, w), mid[j][1, k].reshape(LAT, w))
            sp = dot(polp[k], xin)
            dm = damp[:, d0:d0 + w]
            sc = (sp * pair(dm, dm)).astype(jnp.bfloat16)
            fo = dot(polt[k], sc).astype(jnp.bfloat16)
            for part in range(2):
                ret[j][part, k] = fo[:, part * w:(part + 1) * w].reshape(NP, 16, w)
            return 0

        lax.fori_loop(0, 2, body, 0)

    def perm2(j):
        w = CHUNKS[j]

        def body(g, _):
            r0 = pl.multiple_of(g * 16, 16)
            xin = pair(
                pr2[j][pl.ds(g * 8, 8), 0].reshape(256, w),
                pr2[j][pl.ds(g * 8, 8), 1].reshape(256, w),
            )
            yo = dot(q2[...], xin).astype(jnp.bfloat16)
            for part in range(2):
                zs2[j][:, :, pl.ds(r0 + part * 64, 16), :] = yo[:, part * w:(part + 1) * w].reshape(8, 2, 16, w)
            return 0

        lax.fori_loop(0, 4, body, 0)

    def inverse(j):
        w = CHUNKS[j]
        d0 = offs[j]

        def body(i, _):
            m = pl.multiple_of(i * 256, 256)
            rows = inv[pl.ds(m, 256), :]
            rec = dot(rows, pair(fin[j][:, 0].reshape(N, w), fin[j][:, 1].reshape(N, w))) * (1.0 / 512.0)
            for t in range(2):
                old = airv[j][t, pl.ds(m, 256), :].astype(jnp.float32)
                sea = seab[t, pl.ds(m, 256), :]
                sea = jnp.concatenate([sea] * (w // 128), axis=1)
                new = old + rec[:, t * w:(t + 1) * w] + sea * warm_ref[d0:d0 + w][None, :]
                airv[j][t, pl.ds(m, 256), :] = new.astype(jnp.bfloat16)
            return 0

        lax.fori_loop(0, 4, body, 0)
        pltpu.make_async_copy(airv[j], out_hbm.at[:, :, pl.ds(d0, w)], out_sem.at[j]).start()

    def prepare():
        q1[...] = one_hot(256, 256, lambda r, q: (((r & 15) == (q >> 4)) & ((r >> 5) == ((q >> 1) & 7)) & (((r >> 4) & 1) == (q & 1))))
        q2[...] = one_hot(256, 256, lambda q, r: (((r & 15) == (q >> 4)) & ((r >> 5) == ((q >> 1) & 7)) & (((r >> 4) & 1) == (q & 1))))
        ld_pol.wait()
        sel = one_hot(LAT, LAT, lambda r, q: r == true_lat(q))
        selt = one_hot(LAT, LAT, lambda r, q: true_lat(r) == q)
        for k in range(2):
            polp[k] = dot(pol[k], sel).astype(jnp.bfloat16)
            polt[k] = lax.dot_general(
                selt, pol[k], (((1,), (1,)), ((), ())), preferred_element_type=jnp.float32
            ).astype(jnp.bfloat16)
        eye[...] = one_hot(256, 256, lambda r, q: r == q)

        def turn(i, _):
            r0 = pl.multiple_of((i // 4) * 256, 256)
            n0 = pl.multiple_of(lax.rem(i, 4) * 256, 256)
            inv[pl.ds(n0, 256), pl.ds(r0, 256)] = dot_t(
                eye[...], fwd[pl.ds(r0, 256), pl.ds(n0, 256)]
            ).astype(jnp.bfloat16)
            return 0

        lax.fori_loop(0, 16, turn, 0)
        ld_damp.wait()

    last = nchunk - 1
    ld_fwd.wait()
    ld_air[0].wait()
    dft(0)
    pl.semaphore_wait(barrier, NZ - 1 + NP - 1)
    z_start(0, 0, zs1[0], zr1[0])
    surface_flux()
    flip_copy(0, fpair).start()
    for j in range(1, nchunk):
        dft(j)
        if j < START:
            z_start(0, j, zs1[j], zr1[j])
    flip_copy(0, fpair).wait()
    spread_start(0, fpair, fall)
    prepare()
    find_routes()
    ocean_prepare()

    def step_a(j):
        z_wait(0, j, zs1[j], zr1[j])
        for e in range(START if j == 0 else j + WINDOW, min(j + WINDOW, last) + 1):
            z_start(0, e, zs1[e], zr1[e])
        perm1(j)
        p_start(1, j, ps1[j], mid[j])

    def step_b(j):
        p_wait(1, j, ps1[j], mid[j])
        middle(j)
        p_start(2, j, ret[j], pr2[j])

    def step_c(j):
        p_wait(2, j, pr2[j], pr2[j])
        perm2(j)
        z_start(3, j, zs2[j], fin[j])

    def step_d(j):
        z_wait(3, j, zs2[j], fin[j])
        inverse(j)

    for i in range(nchunk + LAG):
        if i < nchunk:
            step_a(i)
        if i == OCEAN_AT:
            ocean_all()
        if i == OCEAN_AT + 1:
            flip_copy(1, spair).wait()
            spread_start(1, spair, sall)
        if 0 <= i - 1 < nchunk:
            step_b(i - 1)
        if 0 <= i - 2 < nchunk:
            step_c(i - 2)
        if i == LAG:
            place_sea()
        if 0 <= i - LAG < nchunk:
            step_d(i - LAG)

    spread_sent(0, fall)
    spread_sent(1, sall)
    pltpu.make_async_copy(ocean, ocean_hbm, xs_sem.at[0, 5]).wait()
    for j in range(nchunk):
        z_sent(0, j, zs1[j], zr1[j])
        p_sent(1, j, ps1[j])
        p_sent(2, j, pr2[j])
        z_sent(3, j, zs2[j], fin[j])
        pltpu.make_async_copy(airv[j], out_hbm.at[:, :, pl.ds(offs[j], CHUNKS[j])], out_sem.at[j]).wait()


def spectral(air, fwd, pol, damp, patch, *rest):
    bf = jnp.bfloat16
    n = len(CHUNKS)
    scratch = [
        pltpu.VMEM((N, N), bf), pltpu.VMEM((N, N), bf),
        pltpu.VMEM((2, LAT, LAT), bf), pltpu.VMEM((2, LAT, LAT), bf), pltpu.VMEM((2, LAT, LAT), bf),
        pltpu.VMEM((LAT, 768), jnp.float32), pltpu.VMEM((256, 256), bf), pltpu.VMEM((256, 256), bf),
    ]
    scratch += [pltpu.VMEM((2, N, w), bf) for w in CHUNKS]
    scratch += [pltpu.VMEM((NZ, 2, 128, w), bf) for w in CHUNKS]
    scratch += [pltpu.VMEM((NZ, 2, 128, w), bf) for w in CHUNKS]
    scratch += [pltpu.VMEM((NP, 2, 2, 16, w), bf) for w in CHUNKS]
    scratch += [pltpu.VMEM((2, 2, NP, 16, w), bf) for w in CHUNKS]
    scratch += [pltpu.VMEM((2, 2, NP, 16, w), bf) for w in CHUNKS]
    scratch += [pltpu.VMEM((NP, 2, 2, 16, w), bf) for w in CHUNKS]
    scratch += [pltpu.VMEM((NZ, 2, 128, w), bf) for w in CHUNKS]
    scratch += [pltpu.VMEM((NZ, 2, 128, w), bf) for w in CHUNKS]
    scratch += [
        pltpu.VMEM((6, 1032, 128), bf), pltpu.VMEM((6, 4, 264, 128), jnp.float32),
        pltpu.VMEM((256, 256), bf), pltpu.VMEM((32, 256), bf),
        pltpu.VMEM((2, 4, 2, 8, 256), bf), pltpu.VMEM((16, 2, 4, 2, 8, 256), bf),
        pltpu.VMEM((2, 16, 256), bf), pltpu.VMEM((16, 2, 16, 256), bf),
        pltpu.VMEM((2, N, 128), jnp.float32), pltpu.VMEM((6, 512, 128), bf),
        pltpu.VMEM((128, 1152), bf), pltpu.VMEM((128, 128), bf), pltpu.VMEM((128, 8), bf),
        pltpu.VMEM((256, 256), bf), pltpu.VMEM((512, 512), bf), pltpu.SMEM((16,), jnp.int32),
    ]
    dma = pltpu.SemaphoreType.DMA
    scratch += [dma((4 + n,)), dma((n,)), dma((4, n)), dma((4, n)), dma((4, n)), dma((2, 6))]
    anys = pl.BlockSpec(memory_space=pl.ANY)
    vm = pl.BlockSpec(memory_space=pltpu.VMEM)
    sm = pl.BlockSpec(memory_space=pltpu.SMEM)
    return pl.pallas_call(
        spectral_kernel,
        out_shape=(jax.ShapeDtypeStruct(air.shape, bf), jax.ShapeDtypeStruct((6, 512, 128), bf)),
        in_specs=[anys] * 5 + [vm] * 8 + [sm] * 2,
        out_specs=(anys, anys),
        scratch_shapes=scratch,
        compiler_params=pltpu.CompilerParams(
            collective_id=0, has_side_effects=True, vmem_limit_bytes=60 << 20
        ),
        name="spectral",
    )(air, fwd, pol, damp, patch, *rest)


def hand_over_kernel(air_in, ocean_in, air_out, ocean_out, air_buf, ocean_buf, in_sems, out_sems):
    rows = 2 * N // PIECES
    spots = [(air_in, air_buf, air_out, pl.ds(m * rows, rows)) for m in range(PIECES)]
    spots += [(ocean_in, ocean_buf, ocean_out, pl.ds(m * 2, 2)) for m in range(3)]
    reads = [pltpu.make_async_copy(a.at[r], v.at[r], in_sems.at[i]) for i, (a, v, o, r) in enumerate(spots)]
    writes = [pltpu.make_async_copy(v.at[r], o.at[r], out_sems.at[i]) for i, (a, v, o, r) in enumerate(spots)]
    for copy in reads:
        copy.start()
    for read, write in zip(reads, writes):
        read.wait()
        write.start()
    for copy in writes:
        copy.wait()


def hand_over(air, ocean):
    anys = pl.BlockSpec(memory_space=pl.ANY)
    air2, ocean2 = air.reshape(2 * N, -1), ocean
    a, o = pl.pallas_call(
        hand_over_kernel,
        out_shape=tuple(jax.ShapeDtypeStruct(v.shape, v.dtype) for v in (air2, ocean2)),
        in_specs=[anys] * 2,
        out_specs=(anys, anys),
        scratch_shapes=[
            pltpu.VMEM(air2.shape, air2.dtype), pltpu.VMEM(ocean2.shape, ocean2.dtype),
            pltpu.SemaphoreType.DMA((PIECES + 3,)), pltpu.SemaphoreType.DMA((PIECES + 3,)),
        ],
        compiler_params=pltpu.CompilerParams(vmem_limit_bytes=60 << 20),
        name="hand_over",
    )(air2, ocean2)
    o = o.reshape(6, 128, 2, 2, 128).transpose(0, 1, 3, 2, 4).reshape(6, 128, 2, 256)
    return a.reshape(air.shape), o


def shards(
    air_field_lattice,
    associated_polynomial_matrix,
    harmonic_damping_factor,
    boundary_exchange_projector,
    warmth_response_factor,
    water_patch_fields,
    kernel_coefficients,
    local_exchange_matrix,
    patch_average_matrix,
    water_kernel_offset,
    water_readout_matrix,
    patch_holder_index,
    water_point_indicator,
    water_point_totals,
):
    advanced, ocean = spectral(
        air_field_lattice,
        jnp.asarray(basis_table()),
        associated_polynomial_matrix,
        harmonic_damping_factor,
        water_patch_fields.transpose(0, 3, 2, 1).reshape(6, 1032, 128),
        warmth_response_factor,
        boundary_exchange_projector.T,
        kernel_coefficients.reshape(9 * 128, 128),
        local_exchange_matrix,
        patch_average_matrix,
        water_kernel_offset[None, :],
        water_readout_matrix,
        water_point_indicator,
        water_point_totals,
        patch_holder_index.T,
    )
    return hand_over(advanced, ocean)


def solution(mesh):
    placed = (
        P(("sec", "band", "ch"), None, None),
        P(("sec", "band", "ch"), None, None),
        P(),
        P(),
        P(),
        P(("sec", "band", "ch"), None, None, None),
        P(),
        P(),
        P(),
        P(),
        P(),
        P(),
        P(("sec", "band", "ch"), None, None),
        P(("sec", "band", "ch")),
    )
    return jax.shard_map(
        shards,
        mesh=mesh,
        in_specs=placed,
        out_specs=(
            P(("sec", "band", "ch"), None, None),
            P(("sec", "band", "ch"), None, None, None),
        ),
        check_vma=False,
    )
```

```python
import functools
import math

import jax
import jax.numpy as jnp
import numpy as np
from jax import lax
from jax.experimental import pallas as pl
from jax.experimental.pallas import tpu as pltpu
from jax.sharding import PartitionSpec as P

MESH = pl.DeviceIdType.MESH
CHUNKS = (128,) * 6
WINDOW = 3
LAG = 4
OCEAN_AT = 1
START = 3
PIECES = 8
HAND = 1
NZ, NY, NX, NC = 8, 4, 4, 2
NP = NY * NX * NC
N = 1024
LAT = 512


def basis_table():
    z_hi, z_lo, part, y, low = np.meshgrid(
        np.arange(2), np.arange(4), np.arange(2), np.arange(4), np.arange(16), indexing="ij"
    )
    k = (z_lo * 128 + y * 32 + z_hi * 16 + low).reshape(-1)[:, None]
    angle = ((k * np.arange(N)[None, :]) % N).astype(np.float64) * (2.0 * math.pi / N)
    table = np.where(part.reshape(-1)[:, None] == 0, np.cos(angle), -np.sin(angle))
    return table.astype(np.float32).astype(jnp.bfloat16)


def one_hot(rows, cols, fn):
    r = lax.broadcasted_iota(jnp.int32, (rows, cols), 0)
    c = lax.broadcasted_iota(jnp.int32, (rows, cols), 1)
    return jnp.where(fn(r, c), 1.0, 0.0).astype(jnp.bfloat16)


def true_lat(i):
    t = i & 1
    z_lo = (i >> 1) & 3
    z_hi = (i >> 3) & 1
    c = (i >> 4) & 1
    x = (i >> 5) & 3
    y = (i >> 7) & 3
    return (z_lo * 64 + y * 16 + z_hi * 8 + x * 2 + c) * 2 + t


def spectral_kernel(
    air_hbm, fwd_hbm, pol_hbm, damp_hbm, patch_hbm, warm_ref, proj_ref, conv_ref,
    local_ref, mean_ref, bias_ref, read_ref, wet_ref, total_ref, owner_ref,
    out_hbm, ocean_hbm, *scr
):
    nchunk = len(CHUNKS)
    it = iter(scr)
    fwd, inv, pol, polp, polt, damp, q1, q2 = (next(it) for _ in range(8))
    airv = [next(it) for _ in CHUNKS]
    zs1 = [next(it) for _ in CHUNKS]
    zr1 = [next(it) for _ in CHUNKS]
    ps1 = [next(it) for _ in CHUNKS]
    mid = [next(it) for _ in CHUNKS]
    ret = [next(it) for _ in CHUNKS]
    pr2 = [next(it) for _ in CHUNKS]
    zs2 = [next(it) for _ in CHUNKS]
    fin = [next(it) for _ in CHUNKS]
    patch, x3, q3, q4, fpair, fall, spair, sall, seab, ocean = (next(it) for _ in range(10))
    conv_t, read_t, local_t, eye, q5, route = (next(it) for _ in range(6))
    load_sem, out_sem, send_sem, recv_sem, self_sem, xs_sem = (next(it) for _ in range(6))

    s = lax.axis_index("sec")
    b = lax.axis_index("band")
    c = lax.axis_index("ch")
    y = b // 8
    z_hi = lax.rem(b // 4, 2)
    x = lax.rem(b, 4)
    z = z_hi * 4 + s
    p = y * 8 + x * 2 + c
    yx = y * 4 + x

    def z_dev(zz):
        return (lax.rem(zz, 4), y * 8 + (zz // 4) * 4 + x, c)

    def p_dev(pp):
        return (s, (pp // 8) * 8 + z_hi * 4 + lax.rem(pp // 2, 4), lax.rem(pp, 2))

    offs = [0]
    for w in CHUNKS:
        offs.append(offs[-1] + w)

    loads = []

    def load(src, dst):
        copy = pltpu.make_async_copy(src, dst, load_sem.at[len(loads)])
        copy.start()
        loads.append(copy)
        return copy

    ld_fwd = load(fwd_hbm, fwd)
    ld_air = [load(air_hbm.at[:, :, pl.ds(offs[j], CHUNKS[j])], airv[j]) for j in range(nchunk)]
    ld_pol = load(pol_hbm, pol)
    ld_damp = load(damp_hbm, damp)
    ld_patch = load(patch_hbm, patch)

    barrier = pltpu.get_barrier_semaphore()

    def greet_z(i, _):
        pl.semaphore_signal(barrier, inc=1, device_id=z_dev(lax.rem(z + i, NZ)), device_id_type=MESH)
        return 0

    def greet_p(i, _):
        pl.semaphore_signal(barrier, inc=1, device_id=p_dev(lax.rem(p + i, NP)), device_id_type=MESH)
        return 0

    lax.fori_loop(1, NZ, greet_z, 0)
    lax.fori_loop(1, NP, greet_p, 0)

    def z_copy(stage, j, src, dst, i):
        near = (i + 1) // 2
        to = lax.rem(z + jnp.where(lax.rem(i, 2) == 1, near, NZ - near), NZ)
        return pltpu.make_async_remote_copy(
            src_ref=src.at[to], dst_ref=dst.at[z],
            send_sem=send_sem.at[stage, j], recv_sem=recv_sem.at[stage, j],
            device_id=z_dev(to), device_id_type=MESH,
        )

    def z_start(stage, j, src, dst):
        pltpu.make_async_copy(src.at[z], dst.at[z], self_sem.at[stage, j]).start()

        def go(i, _):
            z_copy(stage, j, src, dst, i).start()
            return 0

        lax.fori_loop(1, NZ, go, 0)

    def z_wait(stage, j, src, dst):
        pltpu.make_async_copy(src.at[z], dst.at[z], self_sem.at[stage, j]).wait()
        pltpu.make_async_copy(src.at[pl.ds(0, NZ - 1)], dst.at[pl.ds(0, NZ - 1)], recv_sem.at[stage, j]).wait()

    def z_sent(stage, j, src, dst):
        pltpu.make_async_copy(src.at[pl.ds(0, NZ - 1)], dst.at[pl.ds(0, NZ - 1)], send_sem.at[stage, j]).wait()

    def p_start(stage, j, src, dst):
        def pick(to):
            if stage == 1:
                return src.at[to], dst.at[:, :, p]
            return src.at[:, :, to], dst.at[p]

        a, d = pick(p)
        pltpu.make_async_copy(a, d, self_sem.at[stage, j]).start()

        def go(i, _):
            to = lax.rem(p + i, NP)
            a, d = pick(to)
            pltpu.make_async_remote_copy(
                src_ref=a, dst_ref=d, send_sem=send_sem.at[stage, j], recv_sem=recv_sem.at[stage, j],
                device_id=p_dev(to), device_id_type=MESH,
            ).start()
            return 0

        lax.fori_loop(1, NP, go, 0)

    def p_wait(stage, j, flat, whole):
        a = flat.at[0]
        pltpu.make_async_copy(a, a, self_sem.at[stage, j]).wait()
        a = flat.at[pl.ds(0, NP - 1)]
        pltpu.make_async_copy(a, a, recv_sem.at[stage, j]).wait()

    def p_sent(stage, j, flat):
        a = flat.at[pl.ds(0, NP - 1)]
        pltpu.make_async_copy(a, a, send_sem.at[stage, j]).wait()

    def dot(a, bb):
        return jnp.dot(a, bb, preferred_element_type=jnp.float32)

    def flip_copy(stage, buf):
        return pltpu.make_async_remote_copy(
            src_ref=buf.at[z_hi], dst_ref=buf.at[z_hi], send_sem=xs_sem.at[stage, 0], recv_sem=xs_sem.at[stage, 1],
            device_id=z_dev(lax.rem(z + 4, NZ)), device_id_type=MESH,
        )

    def spread_start(stage, pair, whole):
        pltpu.make_async_copy(pair, whole.at[yx], xs_sem.at[stage, 2]).start()

        def go(i, _):
            to = lax.rem(yx + i, 16)
            pltpu.make_async_remote_copy(
                src_ref=pair, dst_ref=whole.at[yx], send_sem=xs_sem.at[stage, 3], recv_sem=xs_sem.at[stage, 4],
                device_id=p_dev(to * 2 + c), device_id_type=MESH,
            ).start()
            return 0

        lax.fori_loop(1, 16, go, 0)

    def spread_wait(stage, pair, whole):
        pltpu.make_async_copy(pair, whole.at[yx], xs_sem.at[stage, 2]).wait()
        a = whole.at[pl.ds(0, 15)]
        pltpu.make_async_copy(a, a, xs_sem.at[stage, 4]).wait()

    def spread_sent(stage, whole):
        a = whole.at[pl.ds(0, 15)]
        pltpu.make_async_copy(a, a, xs_sem.at[stage, 3]).wait()

    def dot_t(a, bb):
        return lax.dot_general(a, bb, (((1,), (1,)), ((), ())), preferred_element_type=jnp.float32)

    def surface_flux():
        for j in range(nchunk):
            ld_air[j].wait() if j else None
        for t in range(2):
            acc = None
            for j in range(nchunk):
                part = dot_t(proj_ref[:, offs[j]:offs[j] + CHUNKS[j]], airv[j][t])
                acc = part if acc is None else acc + part
            acc = acc.astype(jnp.bfloat16)
            for q in range(4):
                fpair[z_hi, q, t] = acc[:, q * 256:(q + 1) * 256]

    def rows_first(i, _):
        for blk in range(4):
            rows = patch[i, blk * 256:(blk + 1) * 256, :]
            x3[i, :, blk * 64:(blk + 1) * 64, :] = dot(q3[...], rows).reshape(4, 64, 128)
        x3[i, :, 256:264, :] = dot(q4[...], patch[i, 776:1032, :]).reshape(4, 8, 128)
        return 0

    def ocean_step(i, sea):
        tile = route[i]
        owner_b = tile >> 2
        flux = fall[((owner_b >> 3) << 2) + (owner_b & 3), (owner_b >> 2) & 1, tile & 3].astype(jnp.float32)
        wet = wet_ref[i].astype(jnp.float32)
        masked = [flux[r] * wet[r:r + 1, :] for r in range(2)]
        whole = jnp.sum(masked[0] + masked[1], axis=1, keepdims=True)
        fmean = whole / jnp.maximum(total_ref[i].astype(jnp.float32), 1.0)
        row = jnp.sum(mean_ref[...] * fmean, axis=0, keepdims=True) + bias_ref[...]
        shift = jnp.broadcast_to(row, (128, 128)).T
        shift = jnp.concatenate([shift, shift], axis=1)
        fresh = []
        for r in range(2):
            wins = [
                x3[i, r + dr, dw:dw + 256, :].astype(jnp.bfloat16) for dr in range(3) for dw in range(3)
            ]
            pre = dot_t(conv_t[...], jnp.concatenate(wins, axis=1))
            pre = pre + dot(local_t[...], masked[r].astype(jnp.bfloat16)) + shift
            hidden = jax.nn.gelu(pre, approximate=True).astype(jnp.bfloat16)
            old = dot_t(eye[:128, :128], wins[4])
            new = (old + dot(read_t[...], hidden)) * wet[r:r + 1, :]
            fresh.append(new.astype(jnp.bfloat16))
            line = lax.broadcasted_iota(jnp.int32, (16, 256), 0)
            sea = jnp.where(line == 2 * i + r, jnp.broadcast_to(new[0:1, :], (16, 256)), sea)
        quarters = [fresh[r][:, h * 128:(h + 1) * 128] for h in range(2) for r in range(2)]
        ocean[i] = dot(q5[...], jnp.concatenate(quarters, axis=0)).astype(jnp.bfloat16)
        return sea

    def ocean_prepare():
        q3[...] = one_hot(256, 256, lambda r, q: ((r >> 6) == (q & 3)) & ((r & 63) == (q >> 2)))
        q4[...] = one_hot(32, 256, lambda r, q: q == (r & 7) * 4 + (r >> 3) + 248)
        q5[...] = one_hot(512, 512, lambda r, q: ((r >> 2) == (q & 127)) & ((r & 3) == (q >> 7)))
        small = eye[:128, :128]
        conv_t[...] = dot_t(small, conv_ref[...]).astype(jnp.bfloat16)
        read_t[...] = dot_t(small, read_ref[...]).astype(jnp.bfloat16)
        local_t[...] = dot_t(small, local_ref[...]).astype(jnp.bfloat16)
        ld_patch.wait()
        lax.fori_loop(0, 6, rows_first, 0)

    def find_routes():
        mine = [owner_ref[q, (s * 32 + b) * 2 + c] for q in range(4)]

        def scan(i, held):
            held = list(held)
            for q in range(4):
                owner = owner_ref[q, (s * 32 + i) * 2 + c]
                hit = owner == b
                for k in range(6):
                    held[k] = jnp.where(hit & (held[6] == k), i * 4 + q, held[k])
                held[6] = held[6] + jnp.where(hit, 1, 0)
                for k in range(4):
                    before = i * 4 + q < b * 4 + k
                    held[7 + k] = held[7 + k] + jnp.where((owner == mine[k]) & before, 1, 0)
            return tuple(held)

        held = lax.fori_loop(0, 32, scan, tuple(jnp.int32(0) for _ in range(11)))
        for k in range(6):
            route[k] = held[k]
        for k in range(4):
            route[8 + k] = mine[k]
            route[12 + k] = held[7 + k]

    def ocean_all():
        spread_wait(0, fpair, fall)
        sea = lax.fori_loop(0, 6, ocean_step, jnp.zeros((16, 256), jnp.float32))
        spair[z_hi] = sea.astype(jnp.bfloat16)
        flip_copy(1, spair).start()
        pltpu.make_async_copy(ocean, ocean_hbm, xs_sem.at[0, 5]).start()

    def place_sea():
        spread_wait(1, spair, sall)
        for q in range(4):
            owner = route[8 + q]
            slot = route[12 + q]
            tile = sall[((owner >> 3) << 2) + (owner & 3), (owner >> 2) & 1].astype(jnp.float32)
            for t in range(2):
                line = lax.broadcasted_iota(jnp.int32, (16, 256), 0)
                row = jnp.sum(jnp.where(line == 2 * slot + t, tile, 0.0), axis=0, keepdims=True)
                seab[t, q * 256:(q + 1) * 256, :] = jnp.broadcast_to(row, (128, 256)).T

    def pair(a, bb):
        return jnp.concatenate([a, bb], axis=1)

    def dft(j):
        w = CHUNKS[j]

        def body(m, _):
            rows = fwd[pl.ds(pl.multiple_of(m * 256, 256), 256), :]
            f = dot(rows, pair(airv[j][0], airv[j][1])).astype(jnp.bfloat16)
            for t in range(2):
                zs1[j][pl.ds(m * 2, 2), t] = f[:, t * w:(t + 1) * w].reshape(2, 128, w)
            return 0

        lax.fori_loop(0, 4, body, 0)

    def perm1(j):
        w = CHUNKS[j]

        def body(g, _):
            r0 = pl.multiple_of(g * 16, 16)
            xin = pair(
                zr1[j][:, :, pl.ds(r0, 16), :].reshape(256, w),
                zr1[j][:, :, pl.ds(r0 + 64, 16), :].reshape(256, w),
            )
            yo = dot(q1[...], xin).astype(jnp.bfloat16)
            for part in range(2):
                ps1[j][pl.ds(g * 8, 8), part] = yo[:, part * w:(part + 1) * w].reshape(8, 2, 16, w)
            return 0

        lax.fori_loop(0, 4, body, 0)

    def middle(j):
        w = CHUNKS[j]
        d0 = offs[j]

        def body(k, _):
            xin = pair(mid[j][0, k].reshape(LAT, w), mid[j][1, k].reshape(LAT, w))
            sp = dot(polp[k], xin)
            dm = damp[:, d0:d0 + w]
            sc = (sp * pair(dm, dm)).astype(jnp.bfloat16)
            fo = dot(polt[k], sc).astype(jnp.bfloat16)
            for part in range(2):
                ret[j][part, k] = fo[:, part * w:(part + 1) * w].reshape(NP, 16, w)
            return 0

        lax.fori_loop(0, 2, body, 0)

    def perm2(j):
        w = CHUNKS[j]

        def body(g, _):
            r0 = pl.multiple_of(g * 16, 16)
            xin = pair(
                pr2[j][pl.ds(g * 8, 8), 0].reshape(256, w),
                pr2[j][pl.ds(g * 8, 8), 1].reshape(256, w),
            )
            yo = dot(q2[...], xin).astype(jnp.bfloat16)
            for part in range(2):
                zs2[j][:, :, pl.ds(r0 + part * 64, 16), :] = yo[:, part * w:(part + 1) * w].reshape(8, 2, 16, w)
            return 0

        lax.fori_loop(0, 4, body, 0)

    def inverse(j):
        w = CHUNKS[j]
        d0 = offs[j]

        def body(i, _):
            m = pl.multiple_of(i * 256, 256)
            rows = inv[pl.ds(m, 256), :]
            rec = dot(rows, pair(fin[j][:, 0].reshape(N, w), fin[j][:, 1].reshape(N, w))) * (1.0 / 512.0)
            for t in range(2):
                old = airv[j][t, pl.ds(m, 256), :].astype(jnp.float32)
                sea = seab[t, pl.ds(m, 256), :]
                sea = jnp.concatenate([sea] * (w // 128), axis=1)
                new = old + rec[:, t * w:(t + 1) * w] + sea * warm_ref[d0:d0 + w][None, :]
                airv[j][t, pl.ds(m, 256), :] = new.astype(jnp.bfloat16)
            return 0

        lax.fori_loop(0, 4, body, 0)
        pltpu.make_async_copy(airv[j], out_hbm.at[:, :, pl.ds(d0, w)], out_sem.at[j]).start()

    def prepare():
        q1[...] = one_hot(256, 256, lambda r, q: (((r & 15) == (q >> 4)) & ((r >> 5) == ((q >> 1) & 7)) & (((r >> 4) & 1) == (q & 1))))
        q2[...] = one_hot(256, 256, lambda q, r: (((r & 15) == (q >> 4)) & ((r >> 5) == ((q >> 1) & 7)) & (((r >> 4) & 1) == (q & 1))))
        ld_pol.wait()
        sel = one_hot(LAT, LAT, lambda r, q: r == true_lat(q))
        selt = one_hot(LAT, LAT, lambda r, q: true_lat(r) == q)
        for k in range(2):
            polp[k] = dot(pol[k], sel).astype(jnp.bfloat16)
            polt[k] = lax.dot_general(
                selt, pol[k], (((1,), (1,)), ((), ())), preferred_element_type=jnp.float32
            ).astype(jnp.bfloat16)
        eye[...] = one_hot(256, 256, lambda r, q: r == q)

        def turn(i, _):
            r0 = pl.multiple_of((i // 4) * 256, 256)
            n0 = pl.multiple_of(lax.rem(i, 4) * 256, 256)
            inv[pl.ds(n0, 256), pl.ds(r0, 256)] = dot_t(
                eye[...], fwd[pl.ds(r0, 256), pl.ds(n0, 256)]
            ).astype(jnp.bfloat16)
            return 0

        lax.fori_loop(0, 16, turn, 0)
        ld_damp.wait()

    last = nchunk - 1
    ld_fwd.wait()
    ld_air[0].wait()
    dft(0)
    pl.semaphore_wait(barrier, NZ - 1 + NP - 1)
    z_start(0, 0, zs1[0], zr1[0])
    surface_flux()
    flip_copy(0, fpair).start()
    for j in range(1, nchunk):
        dft(j)
        if j < START:
            z_start(0, j, zs1[j], zr1[j])
    flip_copy(0, fpair).wait()
    spread_start(0, fpair, fall)
    prepare()
    find_routes()
    ocean_prepare()

    def step_a(j):
        z_wait(0, j, zs1[j], zr1[j])
        for e in range(START if j == 0 else j + WINDOW, min(j + WINDOW, last) + 1):
            z_start(0, e, zs1[e], zr1[e])
        perm1(j)
        p_start(1, j, ps1[j], mid[j])

    def step_b(j):
        p_wait(1, j, ps1[j], mid[j])
        middle(j)
        p_start(2, j, ret[j], pr2[j])

    def step_c(j):
        p_wait(2, j, pr2[j], pr2[j])
        perm2(j)
        z_start(3, j, zs2[j], fin[j])

    def step_d(j):
        z_wait(3, j, zs2[j], fin[j])
        inverse(j)

    for i in range(nchunk + LAG):
        if i < nchunk:
            step_a(i)
        if 0 <= i - 1 < nchunk:
            step_b(i - 1)
        if 0 <= i - 2 < nchunk:
            step_c(i - 2)
        if i == OCEAN_AT:
            ocean_all()
        if i == OCEAN_AT + 1:
            flip_copy(1, spair).wait()
            spread_start(1, spair, sall)
        if i == LAG:
            place_sea()
        if 0 <= i - LAG < nchunk:
            step_d(i - LAG)

    spread_sent(0, fall)
    spread_sent(1, sall)
    pltpu.make_async_copy(ocean, ocean_hbm, xs_sem.at[0, 5]).wait()
    for j in range(nchunk):
        z_sent(0, j, zs1[j], zr1[j])
        p_sent(1, j, ps1[j])
        p_sent(2, j, pr2[j])
        z_sent(3, j, zs2[j], fin[j])
        pltpu.make_async_copy(airv[j], out_hbm.at[:, :, pl.ds(offs[j], CHUNKS[j])], out_sem.at[j]).wait()


def spectral(air, fwd, pol, damp, patch, *rest):
    bf = jnp.bfloat16
    n = len(CHUNKS)
    scratch = [
        pltpu.VMEM((N, N), bf), pltpu.VMEM((N, N), bf),
        pltpu.VMEM((2, LAT, LAT), bf), pltpu.VMEM((2, LAT, LAT), bf), pltpu.VMEM((2, LAT, LAT), bf),
        pltpu.VMEM((LAT, 768), jnp.float32), pltpu.VMEM((256, 256), bf), pltpu.VMEM((256, 256), bf),
    ]
    scratch += [pltpu.VMEM((2, N, w), bf) for w in CHUNKS]
    scratch += [pltpu.VMEM((NZ, 2, 128, w), bf) for w in CHUNKS]
    scratch += [pltpu.VMEM((NZ, 2, 128, w), bf) for w in CHUNKS]
    scratch += [pltpu.VMEM((NP, 2, 2, 16, w), bf) for w in CHUNKS]
    scratch += [pltpu.VMEM((2, 2, NP, 16, w), bf) for w in CHUNKS]
    scratch += [pltpu.VMEM((2, 2, NP, 16, w), bf) for w in CHUNKS]
    scratch += [pltpu.VMEM((NP, 2, 2, 16, w), bf) for w in CHUNKS]
    scratch += [pltpu.VMEM((NZ, 2, 128, w), bf) for w in CHUNKS]
    scratch += [pltpu.VMEM((NZ, 2, 128, w), bf) for w in CHUNKS]
    scratch += [
        pltpu.VMEM((6, 1032, 128), bf), pltpu.VMEM((6, 4, 264, 128), jnp.float32),
        pltpu.VMEM((256, 256), bf), pltpu.VMEM((32, 256), bf),
        pltpu.VMEM((2, 4, 2, 8, 256), bf), pltpu.VMEM((16, 2, 4, 2, 8, 256), bf),
        pltpu.VMEM((2, 16, 256), bf), pltpu.VMEM((16, 2, 16, 256), bf),
        pltpu.VMEM((2, N, 128), jnp.float32), pltpu.VMEM((6, 512, 128), bf),
        pltpu.VMEM((128, 1152), bf), pltpu.VMEM((128, 128), bf), pltpu.VMEM((128, 8), bf),
        pltpu.VMEM((256, 256), bf), pltpu.VMEM((512, 512), bf), pltpu.SMEM((16,), jnp.int32),
    ]
    dma = pltpu.SemaphoreType.DMA
    scratch += [dma((4 + n,)), dma((n,)), dma((4, n)), dma((4, n)), dma((4, n)), dma((2, 6))]
    anys = pl.BlockSpec(memory_space=pl.ANY)
    vm = pl.BlockSpec(memory_space=pltpu.VMEM)
    sm = pl.BlockSpec(memory_space=pltpu.SMEM)
    return pl.pallas_call(
        spectral_kernel,
        out_shape=(jax.ShapeDtypeStruct(air.shape, bf), jax.ShapeDtypeStruct((6, 512, 128), bf)),
        in_specs=[anys] * 5 + [vm] * 8 + [sm] * 2,
        out_specs=(anys, anys),
        scratch_shapes=scratch,
        compiler_params=pltpu.CompilerParams(
            collective_id=0, has_side_effects=True, vmem_limit_bytes=60 << 20
        ),
        name="spectral",
    )(air, fwd, pol, damp, patch, *rest)


def hand_over_kernel(air_in, ocean_in, air_out, ocean_out, air_buf, ocean_buf, in_sems, out_sems):
    rows = 2 * N // PIECES
    spots = [(air_in, air_buf, air_out, pl.ds(m * rows, rows)) for m in range(PIECES)]
    spots += [(ocean_in, ocean_buf, ocean_out, pl.ds(m * 2, 2)) for m in range(3)]
    reads = [pltpu.make_async_copy(a.at[r], v.at[r], in_sems.at[i]) for i, (a, v, o, r) in enumerate(spots)]
    writes = [pltpu.make_async_copy(v.at[r], o.at[r], out_sems.at[i]) for i, (a, v, o, r) in enumerate(spots)]
    for copy in reads:
        copy.start()
    for read, write in zip(reads, writes):
        read.wait()
        write.start()
    for copy in writes:
        copy.wait()


def hand_over(air, ocean):
    anys = pl.BlockSpec(memory_space=pl.ANY)
    air2, ocean2 = air.reshape(2 * N, -1), ocean
    a, o = pl.pallas_call(
        hand_over_kernel,
        out_shape=tuple(jax.ShapeDtypeStruct(v.shape, v.dtype) for v in (air2, ocean2)),
        in_specs=[anys] * 2,
        out_specs=(anys, anys),
        scratch_shapes=[
            pltpu.VMEM(air2.shape, air2.dtype), pltpu.VMEM(ocean2.shape, ocean2.dtype),
            pltpu.SemaphoreType.DMA((PIECES + 3,)), pltpu.SemaphoreType.DMA((PIECES + 3,)),
        ],
        compiler_params=pltpu.CompilerParams(vmem_limit_bytes=60 << 20),
        name="hand_over",
    )(air2, ocean2)
    o = o.reshape(6, 128, 2, 2, 128).transpose(0, 1, 3, 2, 4).reshape(6, 128, 2, 256)
    return a.reshape(air.shape), o


def shards(
    air_field_lattice,
    associated_polynomial_matrix,
    harmonic_damping_factor,
    boundary_exchange_projector,
    warmth_response_factor,
    water_patch_fields,
    kernel_coefficients,
    local_exchange_matrix,
    patch_average_matrix,
    water_kernel_offset,
    water_readout_matrix,
    patch_holder_index,
    water_point_indicator,
    water_point_totals,
):
    advanced, ocean = spectral(
        air_field_lattice,
        jnp.asarray(basis_table()),
        associated_polynomial_matrix,
        harmonic_damping_factor,
        water_patch_fields.transpose(0, 3, 2, 1).reshape(6, 1032, 128),
        warmth_response_factor,
        boundary_exchange_projector.T,
        kernel_coefficients.reshape(9 * 128, 128),
        local_exchange_matrix,
        patch_average_matrix,
        water_kernel_offset[None, :],
        water_readout_matrix,
        water_point_indicator,
        water_point_totals,
        patch_holder_index.T,
    )
    return hand_over(advanced, ocean)


def solution(mesh):
    placed = (
        P(("sec", "band", "ch"), None, None),
        P(("sec", "band", "ch"), None, None),
        P(),
        P(),
        P(),
        P(("sec", "band", "ch"), None, None, None),
        P(),
        P(),
        P(),
        P(),
        P(),
        P(),
        P(("sec", "band", "ch"), None, None),
        P(("sec", "band", "ch")),
    )
    return jax.shard_map(
        shards,
        mesh=mesh,
        in_specs=placed,
        out_specs=(
            P(("sec", "band", "ch"), None, None),
            P(("sec", "band", "ch"), None, None, None),
        ),
        check_vma=False,
    )
```
